256 devices in a mesh: grp: 16 (over z, core), pts: 16 (over y, x).
Axes of the slice: x: 4, y: 4, z: 8, core: 2. Of those that a mesh axis runs over, the one named last changes fastest.
Arguments:
- patches: bfloat16 [16, 16, 16384, 128], P('grp', 'pts'), may hold values from -6 to 6
- counts: int32 [16, 16], replicated, may hold values from 1 to 16384, as said below
- pick_slot: int32 [3, 128], replicated, may hold values from 0 to 16383, as said below
- block_owner: int32 [3], replicated, may hold values from 0 to 255, as said below
Outputs:
- factor_rows: bfloat16 [16, 16, 8192, 384], P('grp', 'pts')
- residual_gain: float32 [16, 16, 8192], P('grp', 'pts')
The draws below stay inside these ranges and needn't reach their ends.
Inputs may be any that keep to these rules, and one draw needn't show every extreme that they name: `counts`: each row sums to 131072, and in every row one device holds exactly 16384; in the last row it is the last column. `pick_slot`: the 128 slots of round r are distinct and below the count of block_owner[r]; the round owned by the last device includes slot 16383. `block_owner`: the owners of the rounds are distinct devices, and one of them is the last device.
All inputs are finite; a program needn't handle non-finite values.
Results may differ from the reference program's by a relative error of at most 0.0075.
Values may be sent and summed in bfloat16 or wider, within the bound.
A program may use at most 192 MiB of HBM per device.

```python
import jax
import jax.numpy as jnp
from jax import lax

EMBED = 128
BLOCK = 128
ROUNDS = 3
PTS_DEV = 8192
SLOTS = 16384
FACTOR = 384
N_GRP = 16
N_PTS = 16


def share_table(key):
    heavy_slot = jax.random.randint(jax.random.fold_in(key, 11), (N_PTS,), 0, N_GRP)
    heavy_slot = heavy_slot.at[N_PTS - 1].set(N_GRP - 1)
    weights = jax.random.randint(jax.random.fold_in(key, 12), (N_PTS, N_GRP), 2, 5)
    is_heavy = jnp.arange(N_GRP)[None, :] == heavy_slot[:, None]
    weights = jnp.where(is_heavy, 0, weights)
    remain = (N_GRP - 2) * PTS_DEV
    weight_sum = jnp.sum(weights, axis=1, keepdims=True)
    floor_share = weights * remain // weight_sum
    missing = remain - jnp.sum(floor_share, axis=1, keepdims=True)
    light_order = jnp.cumsum(jnp.where(is_heavy, 0, 1), axis=1)
    extra_one = jnp.where(is_heavy, 0, (light_order <= missing).astype(jnp.int32))
    return jnp.where(is_heavy, 2 * PTS_DEV, floor_share + extra_one).astype(jnp.int32)


def pick_plan(key):
    table = share_table(key)
    device_count = N_GRP * N_PTS
    others = jax.random.permutation(jax.random.fold_in(key, 21), device_count - 1)[:ROUNDS - 1].astype(jnp.int32)
    raw_owners = jnp.concatenate([others, jnp.full((1,), device_count - 1, jnp.int32)])
    order = jax.random.permutation(jax.random.fold_in(key, 23), ROUNDS)
    owners = raw_owners[order].astype(jnp.int32)
    owner_count = table[owners % N_PTS, owners // N_PTS]
    slot_total = 2 * PTS_DEV
    positions = jnp.arange(slot_total, dtype=jnp.int32)[None, :]
    scores = jax.random.randint(jax.random.fold_in(key, 22), (ROUNDS, slot_total), 0, 16384) * slot_total + positions
    scores = jnp.where(positions < owner_count[:, None], scores, scores + 2 ** 29)
    is_last = (owners == device_count - 1)[:, None] & (positions == slot_total - 1)
    scores = jnp.where(is_last, -1, scores)
    chosen_slots = jnp.argsort(scores, axis=1, stable=True)[:, :BLOCK].astype(jnp.int32)
    return (owners, chosen_slots)


def draw_counts(key, part):
    return share_table(key)


def draw_pick_slot(key, part):
    return pick_plan(key)[1]


def draw_block_owner(key, part):
    return pick_plan(key)[0]


def steps_of(stream_key, extent, split, least, high):
    factor_of = 1.0
    for position, parts in split:
        heights = jax.random.uniform(jax.random.fold_in(jax.random.fold_in(stream_key, 6), position), (parts,), jnp.float32, least / len(split), high / len(split))
        factor_of = factor_of * jnp.repeat(jnp.exp(heights), extent[position] // parts).reshape((-1,) + (1,) * (len(extent) - 1 - position))
    return factor_of


def noise(own_key, extent, spread, bound, split=(), kind=jnp.bfloat16):
    entries = jax.random.normal(own_key, extent, jnp.float32) * spread
    if len(split) > 0:
        entries = steps_of(own_key, extent, split, -0.22, 0.18) * entries
    return jnp.clip(entries, min=-bound, max=bound).astype(kind)


def setup_inputs(seed: int = 0) -> dict:
    key_list = jax.random.split(jax.random.key(seed), 5)
    patches = noise(key_list[0], (N_GRP, N_PTS, SLOTS, EMBED), 1.0, 6.0, ((0, 16), (1, 16)))
    counts = draw_counts(jax.random.fold_in(key_list[4], 71), 0)
    pick_slot = draw_pick_slot(jax.random.fold_in(key_list[4], 71), 0)
    block_owner = draw_block_owner(jax.random.fold_in(key_list[4], 71), 0)
    return dict(patches=patches, counts=counts, pick_slot=pick_slot, block_owner=block_owner)


JITTER = 0.1
HIGHEST = lax.Precision.HIGHEST

def squares(matrix):
    return jnp.sum(jnp.square(matrix.astype(jnp.float32)), axis=1)

def affinity(row_data, rows_sq, row_ids, block_rows, block_sq, block_ids):
    cross_dot = lax.dot_general(row_data.astype(jnp.float32), block_rows.astype(jnp.float32), (((1,), (1,)), ((), ())), preferred_element_type=jnp.float32)
    inverse_scale = 1.0 / row_data.shape[1]
    distance = rows_sq[:, None] + block_sq[None, :] - 2.0 * cross_dot
    same_point = (row_ids[:, None] == block_ids[None, :]).astype(jnp.float32)
    return jnp.exp(-inverse_scale * distance) + JITTER * same_point

def extend(factors, kernel_part, cross_rows, inverse):
    if factors.shape[1] > 0:
        kernel_part = kernel_part - lax.dot_general(factors.astype(jnp.float32), cross_rows.astype(jnp.float32), (((1,), (1,)), ((), ())), precision=HIGHEST, preferred_element_type=jnp.float32)
    fresh_rows = lax.dot_general(kernel_part.astype(jnp.float32), inverse.astype(jnp.float32), (((1,), (1,)), ((), ())), precision=HIGHEST, preferred_element_type=jnp.float32)
    return jnp.concatenate([factors, fresh_rows], axis=1)

def prepare(blocks, block_ids):
    round_count, block_size = block_ids.shape
    stacked = blocks.reshape(round_count * block_size, blocks.shape[2])
    stacked_ids = block_ids.reshape(-1)
    stacked_sq = squares(stacked)
    factors = jnp.zeros((round_count * block_size, 0), jnp.float32)
    identity = jnp.eye(block_size, dtype=jnp.float32)
    inverses = []
    crosses = []
    for step_index in range(round_count):
        lower_edge = step_index * block_size
        cross_rows = factors[lower_edge:lower_edge + block_size]
        block_sq = stacked_sq[lower_edge:lower_edge + block_size]
        schur_block = affinity(blocks[step_index], block_sq, block_ids[step_index], blocks[step_index], block_sq, block_ids[step_index])
        if step_index > 0:
            schur_block = schur_block - lax.dot_general(cross_rows.astype(jnp.float32), cross_rows.astype(jnp.float32), (((1,), (1,)), ((), ())), precision=HIGHEST, preferred_element_type=jnp.float32)
        factor_low = jnp.linalg.cholesky(schur_block)
        inverse = lax.linalg.triangular_solve(factor_low, identity, left_side=True, lower=True)
        kernel_part = affinity(stacked, stacked_sq, stacked_ids, blocks[step_index], block_sq, block_ids[step_index])
        factors = extend(factors, kernel_part, cross_rows, inverse)
        inverses.append(inverse)
        crosses.append(cross_rows)
    return (inverses, crosses)

def factorize(row_data, row_ids, blocks, block_ids, inverses, crosses):
    rows_sq = squares(row_data)
    blocks_sq = squares(blocks.reshape(-1, blocks.shape[2])).reshape(block_ids.shape)
    factors = jnp.zeros((row_data.shape[0], 0), jnp.float32)
    for step_index in range(len(inverses)):
        kernel_part = affinity(row_data, rows_sq, row_ids, blocks[step_index], blocks_sq[step_index], block_ids[step_index])
        factors = extend(factors, kernel_part, crosses[step_index], inverses[step_index])
    point_gains = 1.0 + JITTER - jnp.sum(factors * factors, axis=1)
    return (factors, point_gains)

def reference(patches, counts, pick_slot, block_owner):
    ends_table = jnp.cumsum(counts, axis=1)
    starts_table = ends_table - counts
    slot_rank = jnp.arange(PTS_DEV, dtype=jnp.int32)[None, :] * N_GRP + jnp.arange(N_GRP, dtype=jnp.int32)[:, None]

    def regroup(column_index):
        col_ends = ends_table[column_index]
        col_starts = starts_table[column_index]
        sources = jnp.sum((col_ends[None, None, :] <= slot_rank[:, :, None]).astype(jnp.int32), axis=2)
        within = slot_rank - col_starts[sources]
        return patches[sources, column_index, within]
    points = lax.map(regroup, jnp.arange(N_PTS, dtype=jnp.int32))
    points = jnp.swapaxes(points, 0, 1).reshape(N_GRP * N_PTS, PTS_DEV, EMBED)
    owner_group = block_owner // N_PTS
    owner_column = block_owner % N_PTS
    blocks = patches[owner_group[:, None], owner_column[:, None], pick_slot]
    pick_rank = starts_table[owner_column, owner_group][:, None] + pick_slot
    block_ids = (pick_rank % N_GRP * N_PTS + owner_column[:, None]) * PTS_DEV + pick_rank // N_GRP
    inverses, crosses = prepare(blocks, block_ids)

    def one_shard(pair):
        row_data, shard_index = pair
        row_ids = shard_index * PTS_DEV + jnp.arange(PTS_DEV, dtype=jnp.int32)
        factors, point_gains = factorize(row_data, row_ids, blocks, block_ids, inverses, crosses)
        return (factors.astype(jnp.bfloat16), point_gains)
    factor_rows, residual_gain = lax.map(one_shard, (points, jnp.arange(N_GRP * N_PTS, dtype=jnp.int32)))
    factor_rows = factor_rows.reshape(N_GRP, N_PTS, PTS_DEV, FACTOR)
    residual_gain = residual_gain.reshape(N_GRP, N_PTS, PTS_DEV)
    return (factor_rows, residual_gain)
```

```python
import functools
import math

import jax
import jax.numpy as jnp
from jax import lax
from jax.experimental import pallas as pl
from jax.experimental.pallas import tpu as pltpu
from jax.sharding import PartitionSpec as P

MESH = pl.DeviceIdType.MESH
HIGHEST = lax.Precision.HIGHEST
JITTER = 0.1
EMBED = 128
BLOCK = 128
ROUNDS = 3
FACTOR = ROUNDS * BLOCK
PARTS = 12
PART_ROWS = FACTOR // PARTS
EXP_SCALE = math.log2(math.e) / EMBED
F32 = jnp.float32
BF16 = jnp.bfloat16


def dot(a, b, precision=None):
    return jnp.dot(a, b, precision=precision, preferred_element_type=F32)


def dot_nt(a, b, precision=None):
    return lax.dot_general(
        a, b, (((1,), (1,)), ((), ())), precision=precision, preferred_element_type=F32
    )


def halves(x):
    high = x.astype(BF16)
    return high, (x - high.astype(F32)).astype(BF16)


def pack_kernel(n_grp, n_pts, counts, owner, slot_ref, x_ref, out_ref, picks_ref, wide, column, total):
    step = pl.program_id(0)
    group, col = lax.axis_index("grp"), lax.axis_index("pts")
    me = group * n_pts + col
    rows = wide.shape[0]
    start = jnp.int32(0)
    for h in range(n_grp):
        start += jnp.where(h < group, counts[col, h], 0)
    wide[...] = x_ref[0, 0].astype(F32)
    for t in range(n_grp):
        first = (t - start) & (n_grp - 1)
        out_ref[t] = wide[pl.ds(first, rows // n_grp, stride=n_grp), :].astype(BF16)

    mine = (owner[0] == me) | (owner[1] == me) | (owner[2] == me)

    @pl.when(step == 0)
    def _():
        total[...] = jnp.zeros_like(total)
        for r in range(ROUNDS):

            @pl.when(owner[r] == me)
            def _():
                column[...] = jnp.broadcast_to(slot_ref[r : r + 1, :], (BLOCK, BLOCK)).T

    @pl.when(mine)
    def _():
        lane = lax.broadcasted_iota(jnp.int32, (BLOCK, BLOCK), 1)
        wanted = column[...] - step * rows
        acc = total[...]
        for c in range(rows // BLOCK):
            hit = (wanted == lane + c * BLOCK).astype(F32).astype(BF16)
            acc += dot(hit, x_ref[0, 0, c * BLOCK : (c + 1) * BLOCK, :])
        total[...] = acc

    @pl.when(step == pl.num_programs(0) - 1)
    def _():
        for r in range(ROUNDS):
            picks_ref[r] = jnp.where(owner[r] == me, total[...], 0.0).astype(BF16)


def pack(patches, counts, pick_slot, block_owner, n_grp, n_pts):
    slots = patches.shape[2]
    steps = 8
    rows = slots // steps
    return pl.pallas_call(
        functools.partial(pack_kernel, n_grp, n_pts),
        grid=(steps,),
        out_shape=(
            jax.ShapeDtypeStruct((n_grp, slots // n_grp, EMBED), BF16),
            jax.ShapeDtypeStruct((ROUNDS, BLOCK, EMBED), BF16),
        ),
        in_specs=[
            pl.BlockSpec(memory_space=pltpu.SMEM),
            pl.BlockSpec(memory_space=pltpu.SMEM),
            pl.BlockSpec((ROUNDS, BLOCK), lambda i: (0, 0)),
            pl.BlockSpec((1, 1, rows, EMBED), lambda i: (0, 0, i, 0)),
        ],
        out_specs=(
            pl.BlockSpec((n_grp, rows // n_grp, EMBED), lambda i: (0, i, 0)),
            pl.BlockSpec((ROUNDS, BLOCK, EMBED), lambda i: (0, 0, 0)),
        ),
        scratch_shapes=[
            pltpu.VMEM((rows, EMBED), F32),
            pltpu.VMEM((BLOCK, BLOCK), jnp.int32),
            pltpu.VMEM((BLOCK, EMBED), F32),
        ],
        name="pack",
    )(counts, block_owner, pick_slot, patches)


def spread_kernel(n_grp, n_pts, in_ref, out_ref, got1, got2, part, gathered, s1, r1, s2, r2, s3, r3):
    group, col = lax.axis_index("grp"), lax.axis_index("pts")
    barrier = pltpu.get_barrier_semaphore()
    for d in range(1, n_grp):
        pl.semaphore_signal(
            barrier, inc=1, device_id=(lax.rem(group + d, n_grp), col), device_id_type=MESH
        )
    for d in range(1, n_pts):
        pl.semaphore_signal(
            barrier, inc=1, device_id=(group, lax.rem(col + d, n_pts)), device_id_type=MESH
        )
    pl.semaphore_wait(barrier, n_grp + n_pts - 2)

    def scatter(d):
        target = lax.rem(group + d, n_grp)
        source = jnp.minimum(target, PARTS - 1)
        return target, pltpu.make_async_remote_copy(
            src_ref=in_ref.at[source],
            dst_ref=got1.at[d - 1],
            send_sem=s1.at[d],
            recv_sem=r1.at[d],
            device_id=(target, col),
            device_id_type=MESH,
        )

    def across(d):
        return pltpu.make_async_remote_copy(
            src_ref=part.at[0],
            dst_ref=got2.at[d - 1],
            send_sem=s2.at[d],
            recv_sem=r2.at[d],
            device_id=(group, lax.rem(col + d, n_pts)),
            device_id_type=MESH,
        )

    def gather(d, owner):
        return pltpu.make_async_remote_copy(
            src_ref=part.at[1],
            dst_ref=gathered.at[owner],
            send_sem=s3.at[d],
            recv_sem=r3.at[d],
            device_id=(lax.rem(group + d, n_grp), col),
            device_id_type=MESH,
        )

    for d in range(1, n_grp):
        target, copy = scatter(d)

        @pl.when(target < PARTS)
        def _():
            copy.start()

    @pl.when(group < PARTS)
    def _():
        for d in range(1, n_grp):
            scatter(d)[1].wait_recv()
        acc = in_ref[jnp.minimum(group, PARTS - 1)].astype(F32)
        for d in range(1, n_grp):
            acc += got1[d - 1].astype(F32)
        part[0] = acc.astype(BF16)
        for d in range(1, n_pts):
            across(d).start()
        for d in range(1, n_pts):
            across(d).wait_recv()
        acc = part[0].astype(F32)
        for d in range(1, n_pts):
            acc += got2[d - 1].astype(F32)
        part[1] = acc.astype(BF16)
        for d in range(1, n_grp):
            gather(d, group).start()
        gathered[group] = part[1]

    for d in range(1, n_grp):
        source = lax.rem(group + n_grp - d, n_grp)

        @pl.when(source < PARTS)
        def _():
            gather(d, source).wait_recv()

    out_ref[...] = gathered[...]

    for d in range(1, n_grp):
        target, copy = scatter(d)

        @pl.when(target < PARTS)
        def _():
            copy.wait_send()

    @pl.when(group < PARTS)
    def _():
        for d in range(1, n_pts):
            across(d).wait_send()
        for d in range(1, n_grp):
            gather(d, group).wait_send()


def spread(picks, n_grp, n_pts):
    shape = (PARTS, PART_ROWS, EMBED)
    return pl.pallas_call(
        functools.partial(spread_kernel, n_grp, n_pts),
        out_shape=jax.ShapeDtypeStruct(shape, BF16),
        in_specs=[pl.BlockSpec(memory_space=pltpu.VMEM)],
        out_specs=pl.BlockSpec(memory_space=pltpu.VMEM),
        scratch_shapes=[
            pltpu.VMEM((n_grp - 1,) + shape[1:], BF16),
            pltpu.VMEM((n_pts - 1,) + shape[1:], BF16),
            pltpu.VMEM((2,) + shape[1:], BF16),
            pltpu.VMEM(shape, BF16),
        ]
        + [pltpu.SemaphoreType.DMA((max(n_grp, n_pts),))] * 6,
        compiler_params=pltpu.CompilerParams(collective_id=0, has_side_effects=True),
        cost_estimate=pl.CostEstimate(flops=20_000_000_000, bytes_accessed=200_000, transcendentals=0),
        name="spread",
    )(picks.reshape(shape))


def unit_inverse(a_ref, m_ref):
    sub = lax.broadcasted_iota(jnp.int32, (8, BLOCK), 0)
    m_ref[...] = (
        lax.broadcasted_iota(jnp.int32, (BLOCK, BLOCK), 0)
        == lax.broadcasted_iota(jnp.int32, (BLOCK, BLOCK), 1)
    ).astype(F32)

    def row(x, k):
        return jnp.broadcast_to(x[k : k + 1, :], (8, BLOCK))

    for b in range(BLOCK // 8):
        low = 8 * b
        pa = a_ref[low : low + 8, :]
        pm = m_ref[low : low + 8, :]
        cols = [jnp.broadcast_to(pa[:, low + j : low + j + 1], (8, BLOCK)) for j in range(8)]
        pivots = jnp.ones((8, BLOCK), F32)
        inverses = pivots
        for k in range(8):
            pivot = row(cols[k], k)
            inverse = 1.0 / pivot
            pivots = jnp.where(sub == k, pivot, pivots)
            inverses = jnp.where(sub == k, inverse, inverses)
            if k < 7:
                f = jnp.where(sub > k, cols[k] * inverse, 0.0)
                for j in range(k + 1, 8):
                    cols[j] = cols[j] - f * row(cols[j], k)
                pa = pa - f * row(pa, k)
                pm = pm - f * row(pm, k)
        if b < BLOCK // 8 - 1:
            below = pa.T[low + 8 :, :]
            a_ref[low + 8 :, :] -= dot(below, pa * inverses, HIGHEST)
            m_ref[low + 8 :, :] -= dot(below, pm * inverses, HIGHEST)
        scale = lax.rsqrt(pivots)
        scale = scale * (1.5 - 0.5 * pivots * scale * scale)
        m_ref[low : low + 8, :] = pm * scale


def prepare_kernel(b_ref, high_ref, low_ref, twice_ref, shift_ref, schur, work, inv):
    blocks = b_ref[...]
    wide = blocks.astype(F32)
    sq_high, sq_low = halves(wide * wide)
    ones = jnp.ones((EMBED, BLOCK), BF16)
    sq_col = dot(sq_high, ones) + dot(sq_low, ones)
    row_ones = jnp.ones((8, EMBED), BF16)
    sq_row = (dot_nt(row_ones, sq_high) + dot_nt(row_ones, sq_low))[0:1, :]
    shift_ref[...] = -EXP_SCALE * sq_row
    twice_ref[...] = (2.0 * wide).T.astype(BF16)
    eye = (
        lax.broadcasted_iota(jnp.int32, (BLOCK, BLOCK), 0)
        == lax.broadcasted_iota(jnp.int32, (BLOCK, BLOCK), 1)
    )
    def span(i):
        return slice(i * BLOCK, (i + 1) * BLOCK)

    for i in range(ROUNDS):
        for j in range(i + 1):
            inner = dot_nt(blocks[span(i)], blocks[span(j)])
            dist = 2.0 * inner - sq_col[span(i)] - sq_row[:, span(j)]
            part = jnp.exp2(EXP_SCALE * dist)
            if i == j:
                part = part + jnp.where(eye, JITTER, 0.0)
            schur[i, j] = part

    for r in range(ROUNDS):
        work[...] = schur[r, r]
        unit_inverse(work, inv.at[r, r])
        for i in range(r + 1, ROUNDS):
            schur[i, r] = dot_nt(schur[i, r], inv[r, r], HIGHEST)
        for i in range(r + 1, ROUNDS):
            for j in range(r + 1, i + 1):
                schur[i, j] -= dot_nt(schur[i, r], schur[j, r], HIGHEST)

    inv[1, 0] = -dot(inv[1, 1], dot(schur[1, 0], inv[0, 0], HIGHEST), HIGHEST)
    inv[2, 1] = -dot(inv[2, 2], dot(schur[2, 1], inv[1, 1], HIGHEST), HIGHEST)
    inv[2, 0] = -dot(
        inv[2, 2],
        dot(schur[2, 0], inv[0, 0], HIGHEST) + dot(schur[2, 1], inv[1, 0], HIGHEST),
        HIGHEST,
    )
    for i in range(ROUNDS):
        for j in range(ROUNDS):
            if j <= i:
                high, low = halves(inv[i, j].T)
            else:
                high = low = jnp.zeros((BLOCK, BLOCK), BF16)
            high_ref[span(j), span(i)] = high
            low_ref[span(j), span(i)] = low


def prepare(blocks):
    square = (ROUNDS, ROUNDS, BLOCK, BLOCK)
    return pl.pallas_call(
        prepare_kernel,
        out_shape=(
            jax.ShapeDtypeStruct((FACTOR, FACTOR), BF16),
            jax.ShapeDtypeStruct((FACTOR, FACTOR), BF16),
            jax.ShapeDtypeStruct((EMBED, FACTOR), BF16),
            jax.ShapeDtypeStruct((1, FACTOR), F32),
        ),
        in_specs=[pl.BlockSpec(memory_space=pltpu.VMEM)],
        out_specs=(pl.BlockSpec(memory_space=pltpu.VMEM),) * 4,
        scratch_shapes=[
            pltpu.VMEM(square, F32),
            pltpu.VMEM((BLOCK, BLOCK), F32),
            pltpu.VMEM(square, F32),
        ],
        cost_estimate=pl.CostEstimate(flops=40_000_000_000, bytes_accessed=900_000, transcendentals=0),
        name="prepare",
    )(blocks)


def factor_kernel(
    n_grp, n_pts, chunk, counts, owner, slot_ref, got_ref, high_ref, low_ref, twice_ref, shift_ref,
    out_ref, gain_ref, points, spots,
):
    step = pl.program_id(0)
    rows = out_ref.shape[2]

    @pl.when(step == 0)
    def _():
        group, col = lax.axis_index("grp"), lax.axis_index("pts")
        start = jnp.int32(0)
        for h in range(n_grp):
            count = counts[col, h]
            odd = start & (n_grp - 1)
            begin = lax.div(start, n_grp) + jnp.where(group < odd, 1, 0)
            first = (group - odd) & (n_grp - 1)
            number = jnp.maximum(lax.div(count - first + n_grp - 1, n_grp), 0)

            def move(c, _, h=h, begin=begin):
                at = pl.multiple_of(c * chunk, chunk)
                points[pl.ds(begin + at, chunk), :] = got_ref[h, pl.ds(at, chunk), :].astype(F32)
                return 0

            lax.fori_loop(0, lax.div(number + chunk - 1, chunk), move, 0)
            start += count
        for r in range(ROUNDS):
            own_group, own_col = lax.div(owner[r], n_pts), lax.rem(owner[r], n_pts)
            begin = jnp.int32(0)
            for h in range(n_grp):
                begin += jnp.where(h < own_group, counts[own_col, h], 0)
            rank = begin + slot_ref[r : r + 1, :]
            here = (own_col == col) & ((rank & (n_grp - 1)) == group)
            spots[0:1, r * BLOCK : (r + 1) * BLOCK] = jnp.where(here, rank >> (n_grp.bit_length() - 1), -1)

    base = pl.multiple_of(step * rows, rows)
    wide = points[pl.ds(base, rows), :]
    x = wide.astype(BF16)
    sq = jnp.concatenate(halves(wide * wide), axis=1)
    sq = dot(sq, jnp.ones((2 * EMBED, BLOCK), BF16))
    spot = lax.broadcasted_iota(jnp.int32, (rows, BLOCK), 0) + base
    high, low = [], []
    for r in range(ROUNDS):
        at = slice(r * BLOCK, (r + 1) * BLOCK)
        inner = dot(x, twice_ref[:, at])
        part = jnp.exp2(EXP_SCALE * (inner - sq) + shift_ref[0:1, at])
        part = part + jnp.where(spot == spots[0:1, at], JITTER, 0.0)
        a, b = halves(part)
        high.append(a)
        low.append(b)
    both = 2 * BLOCK
    high01 = jnp.concatenate(high[:2], axis=1)
    low01 = jnp.concatenate(low[:2], axis=1)
    first = (
        dot(high01, high_ref[0:both, :])
        + dot(low01, high_ref[0:both, :])
        + dot(high01, low_ref[0:both, :])
    )
    last = (
        dot(high[2], high_ref[both:, both:])
        + dot(low[2], high_ref[both:, both:])
        + dot(high[2], low_ref[both:, both:])
    )
    parts = [first[:, 0:BLOCK], first[:, BLOCK:both], first[:, both:] + last]
    square = jnp.zeros((rows, BLOCK), F32)
    for r in range(ROUNDS):
        out_ref[0, 0, :, r * BLOCK : (r + 1) * BLOCK] = parts[r].astype(BF16)
        square += parts[r] * parts[r]
    square = jnp.concatenate(halves(square), axis=1)
    gain_ref[...] = (1.0 + JITTER) - dot_nt(jnp.ones((8, 2 * BLOCK), BF16), square)[0:1, :]


def factorize(got, counts, pick_slot, block_owner, high, low, twice, shift, n_grp, n_pts):
    points = got.shape[0] * got.shape[1] // 2
    rows, chunk = 512, 128
    whole = functools.partial(pl.BlockSpec, pipeline_mode=pl.Buffered(1))
    return pl.pallas_call(
        functools.partial(factor_kernel, n_grp, n_pts, chunk),
        grid=(points // rows,),
        out_shape=(
            jax.ShapeDtypeStruct((1, 1, points, FACTOR), BF16),
            jax.ShapeDtypeStruct((1, points), F32),
        ),
        in_specs=[
            pl.BlockSpec(memory_space=pltpu.SMEM),
            pl.BlockSpec(memory_space=pltpu.SMEM),
            whole((ROUNDS, BLOCK), lambda i: (0, 0)),
            whole(got.shape, lambda i: (0, 0, 0)),
            whole((FACTOR, FACTOR), lambda i: (0, 0)),
            whole((FACTOR, FACTOR), lambda i: (0, 0)),
            whole((EMBED, FACTOR), lambda i: (0, 0)),
            whole((1, FACTOR), lambda i: (0, 0)),
        ],
        out_specs=(
            pl.BlockSpec((1, 1, rows, FACTOR), lambda i: (0, 0, i, 0)),
            pl.BlockSpec((1, rows), lambda i: (0, i)),
        ),
        scratch_shapes=[
            pltpu.VMEM((points + chunk, EMBED), F32),
            pltpu.VMEM((1, FACTOR), jnp.int32),
        ],
        compiler_params=pltpu.CompilerParams(vmem_limit_bytes=40 << 20),
        name="factorize",
    )(counts, block_owner, pick_slot, got, high, low, twice, shift)


def per_device(patches, counts, pick_slot, block_owner):
    n_grp, n_pts = lax.axis_size("grp"), lax.axis_size("pts")
    send, picks = pack(patches, counts, pick_slot, block_owner, n_grp, n_pts)
    got = lax.all_to_all(send, "grp", split_axis=0, concat_axis=0, tiled=True)
    blocks = spread(picks, n_grp, n_pts).reshape(FACTOR, EMBED)
    high, low, twice, shift = prepare(blocks)
    rows, gain = factorize(
        got, counts, pick_slot, block_owner, high, low, twice, shift, n_grp, n_pts
    )
    return rows, gain[None]


def solution(mesh):
    in_specs = (P("grp", "pts", None, None), P(), P(), P())
    out_specs = (P("grp", "pts", None, None), P("grp", "pts", None))
    return jax.shard_map(
        per_device, mesh=mesh, in_specs=in_specs, out_specs=out_specs, check_vma=False
    )
```

```python
import functools
import math

import jax
import jax.numpy as jnp
from jax import lax
from jax.experimental import pallas as pl
from jax.experimental.pallas import tpu as pltpu
from jax.sharding import PartitionSpec as P

MESH = pl.DeviceIdType.MESH
HIGHEST = lax.Precision.HIGHEST
JITTER = 0.1
EMBED = 128
BLOCK = 128
ROUNDS = 3
FACTOR = ROUNDS * BLOCK
PARTS = 12
PART_ROWS = FACTOR // PARTS
FIRST_ROWS = 128
EXP_SCALE = math.log2(math.e) / EMBED
F32 = jnp.float32
BF16 = jnp.bfloat16


def dot(a, b, precision=None):
    return jnp.dot(a, b, precision=precision, preferred_element_type=F32)


def dot_nt(a, b, precision=None):
    return lax.dot_general(
        a, b, (((1,), (1,)), ((), ())), precision=precision, preferred_element_type=F32
    )


def halves(x):
    high = x.astype(BF16)
    return high, (x - high.astype(F32)).astype(BF16)


def pack_kernel(n_grp, n_pts, counts, owner, slot_ref, x_ref, out_ref, picks_ref, order, column, total):
    step = pl.program_id(0)
    group, col = lax.axis_index("grp"), lax.axis_index("pts")
    me = group * n_pts + col
    rows = x_ref.shape[2]
    tile = order.shape[0]
    each = tile // n_grp

    @pl.when(step == 0)
    def _():
        start = jnp.int32(0)
        for h in range(n_grp):
            start += jnp.where(h < group, counts[col, h], 0)
        to = lax.broadcasted_iota(jnp.int32, (tile, tile), 0)
        source = (to & (each - 1)) * n_grp + (((to >> (each.bit_length() - 1)) - start) & (n_grp - 1))
        hit = source == lax.broadcasted_iota(jnp.int32, (tile, tile), 1)
        order[...] = hit.astype(F32).astype(BF16)

    for c in range(rows // tile):
        moved = dot(order[...], x_ref[0, 0, c * tile : (c + 1) * tile, :]).astype(BF16)
        out_ref[:, c * each : (c + 1) * each, :] = moved.reshape(n_grp, each, EMBED)

    mine = (owner[0] == me) | (owner[1] == me) | (owner[2] == me)

    @pl.when(step == 0)
    def _():
        total[...] = jnp.zeros_like(total)
        for r in range(ROUNDS):

            @pl.when(owner[r] == me)
            def _():
                column[...] = jnp.broadcast_to(slot_ref[r : r + 1, :], (BLOCK, BLOCK)).T

    @pl.when(mine)
    def _():
        lane = lax.broadcasted_iota(jnp.int32, (BLOCK, BLOCK), 1)
        wanted = column[...] - step * rows
        acc = total[...]
        for c in range(rows // BLOCK):
            hit = (wanted == lane + c * BLOCK).astype(F32).astype(BF16)
            acc += dot(hit, x_ref[0, 0, c * BLOCK : (c + 1) * BLOCK, :])
        total[...] = acc

    @pl.when(step == pl.num_programs(0) - 1)
    def _():
        for r in range(ROUNDS):
            picks_ref[r] = jnp.where(owner[r] == me, total[...], 0.0).astype(BF16)


def pack(patches, counts, pick_slot, block_owner, n_grp, n_pts):
    slots = patches.shape[2]
    steps = 8
    rows = slots // steps
    return pl.pallas_call(
        functools.partial(pack_kernel, n_grp, n_pts),
        grid=(steps,),
        out_shape=(
            jax.ShapeDtypeStruct((n_grp, slots // n_grp, EMBED), BF16),
            jax.ShapeDtypeStruct((ROUNDS, BLOCK, EMBED), BF16),
        ),
        in_specs=[
            pl.BlockSpec(memory_space=pltpu.SMEM),
            pl.BlockSpec(memory_space=pltpu.SMEM),
            pl.BlockSpec((ROUNDS, BLOCK), lambda i: (0, 0)),
            pl.BlockSpec((1, 1, rows, EMBED), lambda i: (0, 0, i, 0)),
        ],
        out_specs=(
            pl.BlockSpec((n_grp, rows // n_grp, EMBED), lambda i: (0, i, 0)),
            pl.BlockSpec((ROUNDS, BLOCK, EMBED), lambda i: (0, 0, 0)),
        ),
        scratch_shapes=[
            pltpu.VMEM((n_grp * 16, n_grp * 16), BF16),
            pltpu.VMEM((BLOCK, BLOCK), jnp.int32),
            pltpu.VMEM((BLOCK, EMBED), F32),
        ],
        name="pack",
    )(counts, block_owner, pick_slot, patches)


def greet(axis_sizes, place):
    barrier = pltpu.get_barrier_semaphore()
    total = 0
    for axis, size in axis_sizes:
        for d in range(1, size):
            pl.semaphore_signal(barrier, inc=1, device_id=place(axis, d), device_id_type=MESH)
        total += size - 1
    pl.semaphore_wait(barrier, total)


def neighbour(n_grp, n_pts):
    group, col = lax.axis_index("grp"), lax.axis_index("pts")

    def place(axis, d):
        if axis == "grp":
            return (lax.rem(group + d, n_grp), col)
        return (group, lax.rem(col + d, n_pts))

    return place


def unit_inverse(a_ref, m_ref):
    sub = lax.broadcasted_iota(jnp.int32, (8, BLOCK), 0)
    m_ref[...] = (
        lax.broadcasted_iota(jnp.int32, (BLOCK, BLOCK), 0)
        == lax.broadcasted_iota(jnp.int32, (BLOCK, BLOCK), 1)
    ).astype(F32)

    def row(x, k):
        return jnp.broadcast_to(x[k : k + 1, :], (8, BLOCK))

    for b in range(BLOCK // 8):
        low = 8 * b
        pa = a_ref[low : low + 8, :]
        pm = m_ref[low : low + 8, :]
        cols = [jnp.broadcast_to(pa[:, low + j : low + j + 1], (8, BLOCK)) for j in range(8)]
        pivots = jnp.ones((8, BLOCK), F32)
        inverses = pivots
        for k in range(8):
            pivot = row(cols[k], k)
            inverse = 1.0 / pivot
            pivots = jnp.where(sub == k, pivot, pivots)
            inverses = jnp.where(sub == k, inverse, inverses)
            if k < 7:
                f = jnp.where(sub > k, cols[k] * inverse, 0.0)
                for j in range(k + 1, 8):
                    cols[j] = cols[j] - f * row(cols[j], k)
                pa = pa - f * row(pa, k)
                pm = pm - f * row(pm, k)
        if b < BLOCK // 8 - 1:
            below = pa.T[low + 8 :, :]
            a_ref[low + 8 :, :] -= dot(below, pa * inverses, HIGHEST)
            m_ref[low + 8 :, :] -= dot(below, pm * inverses, HIGHEST)
        scale = lax.rsqrt(pivots)
        scale = scale * (1.5 - 0.5 * pivots * scale * scale)
        m_ref[low : low + 8, :] = pm * scale


def prepare(blocks, weights_ref, schur, work, inv):
    wide = blocks.astype(F32)
    sq_high, sq_low = halves(wide * wide)
    ones = jnp.ones((EMBED, BLOCK), BF16)
    sq_col = dot(sq_high, ones) + dot(sq_low, ones)
    row_ones = jnp.ones((8, EMBED), BF16)
    sq_row = (dot_nt(row_ones, sq_high) + dot_nt(row_ones, sq_low))[0:1, :]
    weights_ref[2 * FACTOR :, :] = (2.0 * wide).T.astype(BF16)
    eye = (
        lax.broadcasted_iota(jnp.int32, (BLOCK, BLOCK), 0)
        == lax.broadcasted_iota(jnp.int32, (BLOCK, BLOCK), 1)
    )
    def span(i):
        return slice(i * BLOCK, (i + 1) * BLOCK)

    for i in range(ROUNDS):
        for j in range(i + 1):
            inner = dot_nt(blocks[span(i)], blocks[span(j)])
            dist = 2.0 * inner - sq_col[span(i)] - sq_row[:, span(j)]
            part = jnp.exp2(EXP_SCALE * dist)
            if i == j:
                part = part + jnp.where(eye, JITTER, 0.0)
            schur[i, j] = part

    for r in range(ROUNDS):
        work[...] = schur[r, r]
        unit_inverse(work, inv.at[r, r])
        for i in range(r + 1, ROUNDS):
            schur[i, r] = dot_nt(schur[i, r], inv[r, r], HIGHEST)
        for i in range(r + 1, ROUNDS):
            for j in range(r + 1, i + 1):
                schur[i, j] -= dot_nt(schur[i, r], schur[j, r], HIGHEST)

    inv[1, 0] = -dot(inv[1, 1], dot(schur[1, 0], inv[0, 0], HIGHEST), HIGHEST)
    inv[2, 1] = -dot(inv[2, 2], dot(schur[2, 1], inv[1, 1], HIGHEST), HIGHEST)
    inv[2, 0] = -dot(
        inv[2, 2],
        dot(schur[2, 0], inv[0, 0], HIGHEST) + dot(schur[2, 1], inv[1, 0], HIGHEST),
        HIGHEST,
    )
    for i in range(ROUNDS):
        for j in range(ROUNDS):
            if j <= i:
                high, low = halves(inv[i, j].T)
            else:
                high = low = jnp.zeros((BLOCK, BLOCK), BF16)
            weights_ref[span(j), span(i)] = high
            weights_ref[span(ROUNDS + j), span(i)] = low


def exchange_kernel(
    n_grp, n_pts, send_ref, picks_ref, got_ref, weights_ref,
    got1, got2, part, gathered, schur, work, inv, own_sem, *sems,
):
    group, col = lax.axis_index("grp"), lax.axis_index("pts")
    place = neighbour(n_grp, n_pts)
    greet((("pts", n_pts), ("grp", n_grp)), place)
    (s1, r1), (s2, r2), (s3, r3) = sems[0:2], sems[2:4], sems[4:6]
    bulk = sems[6:]
    edges = (0, FIRST_ROWS, send_ref.shape[1])
    order = sorted(range(1, n_grp), key=lambda d: -min(d, n_grp - d))

    def rows(piece, d):
        span = pl.ds(edges[piece], edges[piece + 1] - edges[piece])
        target = lax.rem(group + d, n_grp)
        return pltpu.make_async_remote_copy(
            src_ref=send_ref.at[target, span],
            dst_ref=got_ref.at[group, span],
            send_sem=bulk[2 * piece].at[d],
            recv_sem=bulk[2 * piece + 1].at[d],
            device_id=place("grp", d),
            device_id_type=MESH,
        )

    def scatter(d):
        target = lax.rem(col + d, n_pts)
        return target, pltpu.make_async_remote_copy(
            src_ref=picks_ref.at[jnp.minimum(target, PARTS - 1)],
            dst_ref=got1.at[d - 1],
            send_sem=s1.at[d],
            recv_sem=r1.at[d],
            device_id=place("pts", d),
            device_id_type=MESH,
        )

    def across(d):
        return pltpu.make_async_remote_copy(
            src_ref=part.at[0],
            dst_ref=got2.at[d - 1],
            send_sem=s2.at[d],
            recv_sem=r2.at[d],
            device_id=place("grp", d),
            device_id_type=MESH,
        )

    def gather(d, owner):
        return pltpu.make_async_remote_copy(
            src_ref=part.at[1],
            dst_ref=gathered.at[owner],
            send_sem=s3.at[d],
            recv_sem=r3.at[d],
            device_id=place("pts", d),
            device_id_type=MESH,
        )

    for d in range(1, n_pts):
        target, copy = scatter(d)

        @pl.when(target < PARTS)
        def _():
            copy.start()

    own = pltpu.make_async_copy(send_ref.at[group], got_ref.at[group], own_sem)
    own.start()
    for d in order:
        rows(0, d).start()

    @pl.when(col < PARTS)
    def _():
        acc = picks_ref[jnp.minimum(col, PARTS - 1)].astype(F32)
        for d in range(1, n_pts):
            scatter(d)[1].wait_recv()
            acc += got1[d - 1].astype(F32)
        part[0] = acc.astype(BF16)
        for d in range(1, n_grp):
            across(d).start()

    for d in order:
        rows(1, d).start()

    @pl.when(col < PARTS)
    def _():
        acc = part[0].astype(F32)
        for d in range(1, n_grp):
            across(d).wait_recv()
            acc += got2[d - 1].astype(F32)
        part[1] = acc.astype(BF16)
        for d in range(1, n_pts):
            gather(d, col).start()
        gathered[col] = part[1]

    for d in range(1, n_pts):
        source = lax.rem(col + n_pts - d, n_pts)

        @pl.when(source < PARTS)
        def _():
            gather(d, source).wait_recv()

    prepare(gathered[...].reshape(FACTOR, EMBED), weights_ref, schur, work, inv)

    for d in range(1, n_pts):
        target, copy = scatter(d)

        @pl.when(target < PARTS)
        def _():
            copy.wait_send()

    @pl.when(col < PARTS)
    def _():
        for d in range(1, n_grp):
            across(d).wait_send()
        for d in range(1, n_pts):
            gather(d, col).wait_send()

    own.wait()
    for piece in range(2):
        for d in order:
            rows(piece, d).wait()


def exchange(send, picks, n_grp, n_pts):
    shape = (PARTS, PART_ROWS, EMBED)
    square = (ROUNDS, ROUNDS, BLOCK, BLOCK)
    return pl.pallas_call(
        functools.partial(exchange_kernel, n_grp, n_pts),
        out_shape=(
            jax.ShapeDtypeStruct(send.shape, BF16),
            jax.ShapeDtypeStruct((2 * FACTOR + EMBED, FACTOR), BF16),
        ),
        in_specs=[pl.BlockSpec(memory_space=pltpu.HBM), pl.BlockSpec(memory_space=pltpu.VMEM)],
        out_specs=(pl.BlockSpec(memory_space=pltpu.HBM), pl.BlockSpec(memory_space=pltpu.VMEM)),
        scratch_shapes=[
            pltpu.VMEM((n_pts - 1,) + shape[1:], BF16),
            pltpu.VMEM((n_grp - 1,) + shape[1:], BF16),
            pltpu.VMEM((2,) + shape[1:], BF16),
            pltpu.VMEM(shape, BF16),
            pltpu.VMEM(square, F32),
            pltpu.VMEM((BLOCK, BLOCK), F32),
            pltpu.VMEM(square, F32),
            pltpu.SemaphoreType.DMA,
        ]
        + [pltpu.SemaphoreType.DMA((n,)) for n in (n_pts, n_pts, n_grp, n_grp, n_pts, n_pts)]
        + [pltpu.SemaphoreType.DMA((n_grp,))] * 4,
        compiler_params=pltpu.CompilerParams(
            collective_id=0, has_side_effects=True, vmem_limit_bytes=24 << 20
        ),
        name="exchange",
    )(send, picks.reshape(shape))


def factor_kernel(
    n_grp, n_pts, chunk, counts, owner, slot_ref, got_ref, weights_ref,
    out_ref, gain_ref, points, spots, shift_ref,
):
    step = pl.program_id(0)
    rows = out_ref.shape[2]

    @pl.when(step == 0)
    def _():
        group, col = lax.axis_index("grp"), lax.axis_index("pts")
        start = jnp.int32(0)
        for h in range(n_grp):
            count = counts[col, h]
            odd = start & (n_grp - 1)
            begin = lax.div(start, n_grp) + jnp.where(group < odd, 1, 0)
            first = (group - odd) & (n_grp - 1)
            number = jnp.maximum(lax.div(count - first + n_grp - 1, n_grp), 0)

            def move(c, _, h=h, begin=begin):
                at = pl.multiple_of(c * chunk, chunk)
                points[pl.ds(begin + at, chunk), :] = got_ref[h, pl.ds(at, chunk), :].astype(F32)
                return 0

            lax.fori_loop(0, lax.div(number + chunk - 1, chunk), move, 0)
            start += count
        for r in range(ROUNDS):
            own_group, own_col = lax.div(owner[r], n_pts), lax.rem(owner[r], n_pts)
            begin = jnp.int32(0)
            for h in range(n_grp):
                begin += jnp.where(h < own_group, counts[own_col, h], 0)
            rank = begin + slot_ref[r : r + 1, :]
            here = (own_col == col) & ((rank & (n_grp - 1)) == group)
            spots[0:1, r * BLOCK : (r + 1) * BLOCK] = jnp.where(here, rank >> (n_grp.bit_length() - 1), -1)

        twice = weights_ref[2 * FACTOR :, :].astype(F32)
        twice_high, twice_low = halves(twice * twice)
        ones = jnp.ones((8, EMBED), BF16)
        shift_ref[...] = (-0.25 * EXP_SCALE) * (dot(ones, twice_high) + dot(ones, twice_low))[0:1, :]

    high_ref, low_ref = weights_ref.at[0:FACTOR], weights_ref.at[FACTOR : 2 * FACTOR]
    twice_ref = weights_ref.at[2 * FACTOR :]
    base = pl.multiple_of(step * rows, rows)
    wide = points[pl.ds(base, rows), :]
    x = wide.astype(BF16)
    sq = jnp.concatenate(halves(wide * wide), axis=1)
    sq = dot(sq, jnp.ones((2 * EMBED, BLOCK), BF16))
    spot = lax.broadcasted_iota(jnp.int32, (rows, BLOCK), 0) + base
    high, low = [], []
    for r in range(ROUNDS):
        at = slice(r * BLOCK, (r + 1) * BLOCK)
        inner = dot(x, twice_ref[:, at])
        part = jnp.exp2(EXP_SCALE * (inner - sq) + shift_ref[0:1, at])
        part = part + jnp.where(spot == spots[0:1, at], JITTER, 0.0)
        a, b = halves(part)
        high.append(a)
        low.append(b)
    both = 2 * BLOCK
    high01 = jnp.concatenate(high[:2], axis=1)
    low01 = jnp.concatenate(low[:2], axis=1)
    first = (
        dot(high01, high_ref[0:both, :])
        + dot(low01, high_ref[0:both, :])
        + dot(high01, low_ref[0:both, :])
    )
    last = (
        dot(high[2], high_ref[both:, both:])
        + dot(low[2], high_ref[both:, both:])
        + dot(high[2], low_ref[both:, both:])
    )
    parts = [first[:, 0:BLOCK], first[:, BLOCK:both], first[:, both:] + last]
    square = jnp.zeros((rows, BLOCK), F32)
    for r in range(ROUNDS):
        out_ref[0, 0, :, r * BLOCK : (r + 1) * BLOCK] = parts[r].astype(BF16)
        square += parts[r] * parts[r]
    square = jnp.concatenate(halves(square), axis=1)
    gain_ref[...] = (1.0 + JITTER) - dot_nt(jnp.ones((8, 2 * BLOCK), BF16), square)[0:1, :]


def factorize(got, counts, pick_slot, block_owner, weights, n_grp, n_pts):
    points = got.shape[0] * got.shape[1] // 2
    rows, chunk = 512, 128
    whole = functools.partial(pl.BlockSpec, pipeline_mode=pl.Buffered(1))
    return pl.pallas_call(
        functools.partial(factor_kernel, n_grp, n_pts, chunk),
        grid=(points // rows,),
        out_shape=(
            jax.ShapeDtypeStruct((1, 1, points, FACTOR), BF16),
            jax.ShapeDtypeStruct((1, points), F32),
        ),
        in_specs=[
            pl.BlockSpec(memory_space=pltpu.SMEM),
            pl.BlockSpec(memory_space=pltpu.SMEM),
            whole((ROUNDS, BLOCK), lambda i: (0, 0)),
            whole(got.shape, lambda i: (0, 0, 0)),
            whole(weights.shape, lambda i: (0, 0)),
        ],
        out_specs=(
            pl.BlockSpec((1, 1, rows, FACTOR), lambda i: (0, 0, i, 0)),
            pl.BlockSpec((1, rows), lambda i: (0, i)),
        ),
        scratch_shapes=[
            pltpu.VMEM((points + chunk, EMBED), F32),
            pltpu.VMEM((1, FACTOR), jnp.int32),
            pltpu.VMEM((1, FACTOR), F32),
        ],
        compiler_params=pltpu.CompilerParams(vmem_limit_bytes=40 << 20),
        name="factorize",
    )(counts, block_owner, pick_slot, got, weights)


def per_device(patches, counts, pick_slot, block_owner):
    n_grp, n_pts = lax.axis_size("grp"), lax.axis_size("pts")
    send, picks = pack(patches, counts, pick_slot, block_owner, n_grp, n_pts)
    got, weights = exchange(send, picks, n_grp, n_pts)
    rows, gain = factorize(got, counts, pick_slot, block_owner, weights, n_grp, n_pts)
    return rows, gain[None]


def solution(mesh):
    in_specs = (P("grp", "pts", None, None), P(), P(), P())
    out_specs = (P("grp", "pts", None, None), P("grp", "pts", None))
    return jax.shard_map(
        per_device, mesh=mesh, in_specs=in_specs, out_specs=out_specs, check_vma=False
    )
```

```python
import functools
import math

import jax
import jax.numpy as jnp
from jax import lax
from jax.experimental import pallas as pl
from jax.experimental.pallas import tpu as pltpu
from jax.sharding import PartitionSpec as P

MESH = pl.DeviceIdType.MESH
HIGHEST = lax.Precision.HIGHEST
JITTER = 0.1
EMBED = 128
BLOCK = 128
ROUNDS = 3
FACTOR = ROUNDS * BLOCK
PARTS = 12
PART_ROWS = FACTOR // PARTS
FIRST_ROWS = 256
EXP_SCALE = math.log2(math.e) / EMBED
F32 = jnp.float32
BF16 = jnp.bfloat16


def dot(a, b, precision=None):
    return jnp.dot(a, b, precision=precision, preferred_element_type=F32)


def dot_nt(a, b, precision=None):
    return lax.dot_general(
        a, b, (((1,), (1,)), ((), ())), precision=precision, preferred_element_type=F32
    )


def halves(x):
    high = x.astype(BF16)
    return high, (x - high.astype(F32)).astype(BF16)


def greet(axis_sizes, place, meanwhile):
    barrier = pltpu.get_barrier_semaphore()
    total = 0
    for axis, size in axis_sizes:
        for d in range(1, size):
            pl.semaphore_signal(barrier, inc=1, device_id=place(axis, d), device_id_type=MESH)
        total += size - 1
    meanwhile()
    pl.semaphore_wait(barrier, total)


def neighbour(n_grp, n_pts):
    group, col = lax.axis_index("grp"), lax.axis_index("pts")

    def place(axis, d):
        if axis == "grp":
            return (lax.rem(group + d, n_grp), col)
        return (group, lax.rem(col + d, n_pts))

    return place


def unit_inverse(a_ref, m_ref):
    sub = lax.broadcasted_iota(jnp.int32, (8, BLOCK), 0)
    m_ref[...] = (
        lax.broadcasted_iota(jnp.int32, (BLOCK, BLOCK), 0)
        == lax.broadcasted_iota(jnp.int32, (BLOCK, BLOCK), 1)
    ).astype(F32)

    def row(x, k):
        return jnp.broadcast_to(x[k : k + 1, :], (8, BLOCK))

    for b in range(BLOCK // 8):
        low = 8 * b
        pa = a_ref[low : low + 8, :]
        pm = m_ref[low : low + 8, :]
        cols = [jnp.broadcast_to(pa[:, low + j : low + j + 1], (8, BLOCK)) for j in range(8)]
        pivots = jnp.ones((8, BLOCK), F32)
        inverses = pivots
        for k in range(8):
            pivot = row(cols[k], k)
            inverse = 1.0 / pivot
            pivots = jnp.where(sub == k, pivot, pivots)
            inverses = jnp.where(sub == k, inverse, inverses)
            if k < 7:
                f = jnp.where(sub > k, cols[k] * inverse, 0.0)
                for j in range(k + 1, 8):
                    cols[j] = cols[j] - f * row(cols[j], k)
                pa = pa - f * row(pa, k)
                pm = pm - f * row(pm, k)
        if b < BLOCK // 8 - 1:
            below = pa.T[low + 8 :, :]
            a_ref[low + 8 :, :] -= dot(below, pa * inverses, HIGHEST)
            m_ref[low + 8 :, :] -= dot(below, pm * inverses, HIGHEST)
        scale = lax.rsqrt(pivots)
        scale = scale * (1.5 - 0.5 * pivots * scale * scale)
        m_ref[low : low + 8, :] = pm * scale


def prepare(blocks, weights_ref, schur, work, inv):
    wide = blocks.astype(F32)
    sq_high, sq_low = halves(wide * wide)
    ones = jnp.ones((EMBED, BLOCK), BF16)
    sq_col = dot(sq_high, ones) + dot(sq_low, ones)
    row_ones = jnp.ones((8, EMBED), BF16)
    sq_row = (dot_nt(row_ones, sq_high) + dot_nt(row_ones, sq_low))[0:1, :]
    weights_ref[2 * FACTOR :, :] = (2.0 * wide).T.astype(BF16)
    eye = (
        lax.broadcasted_iota(jnp.int32, (BLOCK, BLOCK), 0)
        == lax.broadcasted_iota(jnp.int32, (BLOCK, BLOCK), 1)
    )
    def span(i):
        return slice(i * BLOCK, (i + 1) * BLOCK)

    for i in range(ROUNDS):
        for j in range(i + 1):
            inner = dot_nt(blocks[span(i)], blocks[span(j)])
            dist = 2.0 * inner - sq_col[span(i)] - sq_row[:, span(j)]
            part = jnp.exp2(EXP_SCALE * dist)
            if i == j:
                part = part + jnp.where(eye, JITTER, 0.0)
            schur[i, j] = part

    for r in range(ROUNDS):
        work[...] = schur[r, r]
        unit_inverse(work, inv.at[r, r])
        for i in range(r + 1, ROUNDS):
            schur[i, r] = dot_nt(schur[i, r], inv[r, r], HIGHEST)
        for i in range(r + 1, ROUNDS):
            for j in range(r + 1, i + 1):
                schur[i, j] -= dot_nt(schur[i, r], schur[j, r], HIGHEST)

    inv[1, 0] = -dot(inv[1, 1], dot(schur[1, 0], inv[0, 0], HIGHEST), HIGHEST)
    inv[2, 1] = -dot(inv[2, 2], dot(schur[2, 1], inv[1, 1], HIGHEST), HIGHEST)
    inv[2, 0] = -dot(
        inv[2, 2],
        dot(schur[2, 0], inv[0, 0], HIGHEST) + dot(schur[2, 1], inv[1, 0], HIGHEST),
        HIGHEST,
    )
    for i in range(ROUNDS):
        for j in range(ROUNDS):
            if j <= i:
                high, low = halves(inv[i, j].T)
            else:
                high = low = jnp.zeros((BLOCK, BLOCK), BF16)
            weights_ref[span(j), span(i)] = high
            weights_ref[span(ROUNDS + j), span(i)] = low


def exchange_kernel(
    n_grp, n_pts, counts, owner, slot_ref, patches_ref, got_ref, weights_ref,
    x_ref, send_ref, order, picks_ref, got1, got2, part, gathered, schur, work, inv,
    load_sems, own_sem, *sems,
):
    group, col = lax.axis_index("grp"), lax.axis_index("pts")
    me = group * n_pts + col
    place = neighbour(n_grp, n_pts)
    (s1, r1), (s2, r2), (s3, r3) = sems[0:2], sems[2:4], sems[4:6]
    bulk = sems[6:]
    per_peer = send_ref.shape[1]
    edges = (0, FIRST_ROWS, per_peer)
    tile = order.shape[0]
    each = tile // n_grp
    loads = load_sems.shape[0]
    load_rows = x_ref.shape[0] // loads
    far_first = sorted(range(1, n_grp), key=lambda d: -min(d, n_grp - d))

    def load(i):
        span = pl.ds(i * load_rows, load_rows)
        return pltpu.make_async_copy(patches_ref.at[0, 0, span], x_ref.at[span], load_sems.at[i])

    for i in range(loads):
        load(i).start()

    def set_order():
        start = jnp.int32(0)
        for h in range(n_grp):
            start += jnp.where(h < group, counts[col, h], 0)
        to = lax.broadcasted_iota(jnp.int32, (tile, tile), 0)
        source = (to & (each - 1)) * n_grp + (((to >> (each.bit_length() - 1)) - start) & (n_grp - 1))
        hit = source == lax.broadcasted_iota(jnp.int32, (tile, tile), 1)
        order[...] = hit.astype(F32).astype(BF16)

    def sort_rows(low, high):
        for c in range(low // each, high // each):
            moved = dot(order[...], x_ref[c * tile : (c + 1) * tile, :]).astype(BF16)
            send_ref[:, c * each : (c + 1) * each, :] = moved.reshape(n_grp, each, EMBED)

    def find_picks():
        slots = jnp.full((1, BLOCK), -1, jnp.int32)
        for r in range(ROUNDS):
            slots = jnp.where(owner[r] == me, slot_ref[r : r + 1, :], slots)
        wanted = jnp.broadcast_to(slots, (BLOCK, BLOCK)).T
        wanted -= lax.broadcasted_iota(jnp.int32, (BLOCK, BLOCK), 1)
        unroll = 8

        def look(i, acc):
            for u in range(unroll):
                at = pl.multiple_of((i * unroll + u) * BLOCK, BLOCK)
                hit = (wanted == at).astype(F32).astype(BF16)
                acc += dot(hit, x_ref[pl.ds(at, BLOCK), :])
            return acc

        found = lax.fori_loop(
            0, x_ref.shape[0] // (unroll * BLOCK), look, jnp.zeros((BLOCK, EMBED), F32)
        )
        for r in range(ROUNDS):
            mine = jnp.where(owner[r] == me, found, 0.0).astype(BF16)
            per_round = BLOCK // PART_ROWS
            picks_ref[r * per_round : (r + 1) * per_round] = mine.reshape(per_round, PART_ROWS, EMBED)

    def rows(piece, d):
        span = pl.ds(edges[piece], edges[piece + 1] - edges[piece])
        target = lax.rem(group + d, n_grp)
        return pltpu.make_async_remote_copy(
            src_ref=send_ref.at[target, span],
            dst_ref=got_ref.at[group, span],
            send_sem=bulk[2 * piece].at[d],
            recv_sem=bulk[2 * piece + 1].at[d],
            device_id=place("grp", d),
            device_id_type=MESH,
        )

    def before():
        set_order()
        for i in range(FIRST_ROWS * n_grp // load_rows):
            load(i).wait()
        sort_rows(0, FIRST_ROWS)

    greet((("pts", n_pts), ("grp", n_grp)), place, before)
    for d in far_first:
        rows(0, d).start()
    for i in range(FIRST_ROWS * n_grp // load_rows, loads):
        load(i).wait()
    find_picks()

    def scatter(d):
        target = lax.rem(col + d, n_pts)
        return target, pltpu.make_async_remote_copy(
            src_ref=picks_ref.at[jnp.minimum(target, PARTS - 1)],
            dst_ref=got1.at[d - 1],
            send_sem=s1.at[d],
            recv_sem=r1.at[d],
            device_id=place("pts", d),
            device_id_type=MESH,
        )

    def across(d):
        return pltpu.make_async_remote_copy(
            src_ref=part.at[0],
            dst_ref=got2.at[d - 1],
            send_sem=s2.at[d],
            recv_sem=r2.at[d],
            device_id=place("grp", d),
            device_id_type=MESH,
        )

    def gather(d, owner):
        return pltpu.make_async_remote_copy(
            src_ref=part.at[1],
            dst_ref=gathered.at[owner],
            send_sem=s3.at[d],
            recv_sem=r3.at[d],
            device_id=place("pts", d),
            device_id_type=MESH,
        )

    for d in range(1, n_pts):
        target, copy = scatter(d)

        @pl.when(target < PARTS)
        def _():
            copy.start()

    sort_rows(FIRST_ROWS, per_peer)
    own = pltpu.make_async_copy(send_ref.at[group], got_ref.at[group], own_sem)
    own.start()

    @pl.when(col < PARTS)
    def _():
        acc = picks_ref[jnp.minimum(col, PARTS - 1)].astype(F32)
        for d in range(1, n_pts):
            scatter(d)[1].wait_recv()
            acc += got1[d - 1].astype(F32)
        part[0] = acc.astype(BF16)
        for d in range(1, n_grp):
            across(d).start()

    for d in far_first:
        rows(1, d).start()

    @pl.when(col < PARTS)
    def _():
        acc = part[0].astype(F32)
        for d in range(1, n_grp):
            across(d).wait_recv()
            acc += got2[d - 1].astype(F32)
        part[1] = acc.astype(BF16)
        for d in range(1, n_pts):
            gather(d, col).start()
        gathered[col] = part[1]

    for d in range(1, n_pts):
        source = lax.rem(col + n_pts - d, n_pts)

        @pl.when(source < PARTS)
        def _():
            gather(d, source).wait_recv()

    prepare(gathered[...].reshape(FACTOR, EMBED), weights_ref, schur, work, inv)

    for d in range(1, n_pts):
        target, copy = scatter(d)

        @pl.when(target < PARTS)
        def _():
            copy.wait_send()

    @pl.when(col < PARTS)
    def _():
        for d in range(1, n_grp):
            across(d).wait_send()
        for d in range(1, n_pts):
            gather(d, col).wait_send()

    own.wait()
    for piece in range(2):
        for d in far_first:
            rows(piece, d).wait()


def exchange(patches, counts, pick_slot, block_owner, n_grp, n_pts):
    slots = patches.shape[2]
    shape = (PARTS, PART_ROWS, EMBED)
    square = (ROUNDS, ROUNDS, BLOCK, BLOCK)
    messages = (n_grp, slots // n_grp, EMBED)
    return pl.pallas_call(
        functools.partial(exchange_kernel, n_grp, n_pts),
        out_shape=(
            jax.ShapeDtypeStruct(messages, BF16),
            jax.ShapeDtypeStruct((2 * FACTOR + EMBED, FACTOR), BF16),
        ),
        in_specs=[
            pl.BlockSpec(memory_space=pltpu.SMEM),
            pl.BlockSpec(memory_space=pltpu.SMEM),
            pl.BlockSpec(memory_space=pltpu.VMEM),
            pl.BlockSpec(memory_space=pltpu.HBM),
        ],
        out_specs=(pl.BlockSpec(memory_space=pltpu.HBM), pl.BlockSpec(memory_space=pltpu.VMEM)),
        scratch_shapes=[
            pltpu.VMEM((slots, EMBED), BF16),
            pltpu.VMEM(messages, BF16),
            pltpu.VMEM((n_grp * 16, n_grp * 16), BF16),
            pltpu.VMEM(shape, BF16),
            pltpu.VMEM((n_pts - 1,) + shape[1:], BF16),
            pltpu.VMEM((n_grp - 1,) + shape[1:], BF16),
            pltpu.VMEM((2,) + shape[1:], BF16),
            pltpu.VMEM(shape, BF16),
            pltpu.VMEM(square, F32),
            pltpu.VMEM((BLOCK, BLOCK), F32),
            pltpu.VMEM(square, F32),
            pltpu.SemaphoreType.DMA((8,)),
            pltpu.SemaphoreType.DMA,
        ]
        + [pltpu.SemaphoreType.DMA((n,)) for n in (n_pts, n_pts, n_grp, n_grp, n_pts, n_pts)]
        + [pltpu.SemaphoreType.DMA((n_grp,))] * 4,
        compiler_params=pltpu.CompilerParams(
            collective_id=0, has_side_effects=True, vmem_limit_bytes=58 << 20
        ),
        name="exchange",
    )(counts, block_owner, pick_slot, patches)


def factor_kernel(
    n_grp, n_pts, chunk, counts, owner, slot_ref, got_ref, weights_ref,
    out_ref, gain_ref, points, spots, shift_ref, doubled,
):
    step = pl.program_id(0)
    rows = out_ref.shape[2]

    @pl.when(step == 0)
    def _():
        group, col = lax.axis_index("grp"), lax.axis_index("pts")
        start = jnp.int32(0)
        for h in range(n_grp):
            count = counts[col, h]
            odd = start & (n_grp - 1)
            begin = lax.div(start, n_grp) + jnp.where(group < odd, 1, 0)
            first = (group - odd) & (n_grp - 1)
            number = jnp.maximum(lax.div(count - first + n_grp - 1, n_grp), 0)

            def move(c, _, h=h, begin=begin):
                at = pl.multiple_of(c * chunk, chunk)
                points[pl.ds(begin + at, chunk), :] = got_ref[h, pl.ds(at, chunk), :].astype(F32)
                return 0

            lax.fori_loop(0, lax.div(number + chunk - 1, chunk), move, 0)
            start += count
        for r in range(ROUNDS):
            own_group, own_col = lax.div(owner[r], n_pts), lax.rem(owner[r], n_pts)
            begin = jnp.int32(0)
            for h in range(n_grp):
                begin += jnp.where(h < own_group, counts[own_col, h], 0)
            rank = begin + slot_ref[r : r + 1, :]
            here = (own_col == col) & ((rank & (n_grp - 1)) == group)
            spots[0:1, r * BLOCK : (r + 1) * BLOCK] = jnp.where(here, rank >> (n_grp.bit_length() - 1), -1)

        corner = weights_ref[2 * BLOCK : FACTOR, 2 * BLOCK :]
        doubled[0:BLOCK, :] = corner
        doubled[BLOCK:, :] = corner
        twice = weights_ref[2 * FACTOR :, :].astype(F32)
        twice_high, twice_low = halves(twice * twice)
        ones = jnp.ones((8, EMBED), BF16)
        shift_ref[...] = (-0.25 * EXP_SCALE) * (dot(ones, twice_high) + dot(ones, twice_low))[0:1, :]

    high_ref, low_ref = weights_ref.at[0:FACTOR], weights_ref.at[FACTOR : 2 * FACTOR]
    twice_ref = weights_ref.at[2 * FACTOR :]
    base = pl.multiple_of(step * rows, rows)
    wide = points[pl.ds(base, rows), :]
    x = wide.astype(BF16)
    sq = jnp.concatenate(halves(wide * wide), axis=1)
    sq = dot(sq, jnp.ones((2 * EMBED, BLOCK), BF16))
    spot = lax.broadcasted_iota(jnp.int32, (rows, BLOCK), 0) + base
    inner = dot(x, twice_ref[...])
    high, low = [], []
    for r in range(ROUNDS):
        at = slice(r * BLOCK, (r + 1) * BLOCK)
        part = jnp.exp2(EXP_SCALE * (inner[:, at] - sq) + shift_ref[0:1, at])
        part = part + jnp.where(spot == spots[0:1, at], JITTER, 0.0)
        a, b = halves(part)
        high.append(a)
        low.append(b)
    both = 2 * BLOCK
    high01 = jnp.concatenate(high[:2], axis=1)
    low01 = jnp.concatenate(low[:2], axis=1)
    first = (
        dot(high01, high_ref[0:both, :])
        + dot(low01, high_ref[0:both, :])
        + dot(high01, low_ref[0:both, :])
    )
    last = (
        dot(jnp.concatenate([high[2], low[2]], axis=1), doubled[...])
        + dot(high[2], low_ref[both:, both:])
    )
    parts = [first[:, 0:BLOCK], first[:, BLOCK:both], first[:, both:] + last]
    square = jnp.zeros((rows, BLOCK), F32)
    for r in range(ROUNDS):
        out_ref[0, 0, :, r * BLOCK : (r + 1) * BLOCK] = parts[r].astype(BF16)
        square += parts[r] * parts[r]
    square = jnp.concatenate(halves(square), axis=1)
    gain_ref[...] = (1.0 + JITTER) - dot_nt(jnp.ones((8, 2 * BLOCK), BF16), square)[0:1, :]


def factorize(got, counts, pick_slot, block_owner, weights, n_grp, n_pts):
    points = got.shape[0] * got.shape[1] // 2
    rows, chunk = 512, 128
    whole = functools.partial(pl.BlockSpec, pipeline_mode=pl.Buffered(1))
    return pl.pallas_call(
        functools.partial(factor_kernel, n_grp, n_pts, chunk),
        grid=(points // rows,),
        out_shape=(
            jax.ShapeDtypeStruct((1, 1, points, FACTOR), BF16),
            jax.ShapeDtypeStruct((1, points), F32),
        ),
        in_specs=[
            pl.BlockSpec(memory_space=pltpu.SMEM),
            pl.BlockSpec(memory_space=pltpu.SMEM),
            whole((ROUNDS, BLOCK), lambda i: (0, 0)),
            whole(got.shape, lambda i: (0, 0, 0)),
            whole(weights.shape, lambda i: (0, 0)),
        ],
        out_specs=(
            pl.BlockSpec((1, 1, rows, FACTOR), lambda i: (0, 0, i, 0)),
            pl.BlockSpec((1, rows), lambda i: (0, i)),
        ),
        scratch_shapes=[
            pltpu.VMEM((points + chunk, EMBED), F32),
            pltpu.VMEM((1, FACTOR), jnp.int32),
            pltpu.VMEM((1, FACTOR), F32),
            pltpu.VMEM((2 * BLOCK, BLOCK), BF16),
        ],
        compiler_params=pltpu.CompilerParams(vmem_limit_bytes=58 << 20),
        name="factorize",
    )(counts, block_owner, pick_slot, got, weights)


def per_device(patches, counts, pick_slot, block_owner):
    n_grp, n_pts = lax.axis_size("grp"), lax.axis_size("pts")
    got, weights = exchange(patches, counts, pick_slot, block_owner, n_grp, n_pts)
    rows, gain = factorize(got, counts, pick_slot, block_owner, weights, n_grp, n_pts)
    return rows, gain[None]


def solution(mesh):
    in_specs = (P("grp", "pts", None, None), P(), P(), P())
    out_specs = (P("grp", "pts", None, None), P("grp", "pts", None))
    return jax.shard_map(
        per_device, mesh=mesh, in_specs=in_specs, out_specs=out_specs, check_vma=False
    )
```

```python
import functools
import math

import jax
import jax.numpy as jnp
from jax import lax
from jax.experimental import pallas as pl
from jax.experimental.pallas import tpu as pltpu
from jax.sharding import PartitionSpec as P

MESH = pl.DeviceIdType.MESH
HIGHEST = lax.Precision.HIGHEST
JITTER = 0.1
EMBED = 128
BLOCK = 128
ROUNDS = 3
FACTOR = ROUNDS * BLOCK
PARTS = 12
PART_ROWS = FACTOR // PARTS
FIRST_ROWS = 256
EARLY_ROWS = 704
SOURCES = 3
EXP_SCALE = math.log2(math.e) / EMBED
F32 = jnp.float32
BF16 = jnp.bfloat16


def dot(a, b, precision=None):
    return jnp.dot(a, b, precision=precision, preferred_element_type=F32)


def dot_nt(a, b, precision=None):
    return lax.dot_general(
        a, b, (((1,), (1,)), ((), ())), precision=precision, preferred_element_type=F32
    )


def halves(x):
    high = x.astype(BF16)
    return high, (x - high.astype(F32)).astype(BF16)


def greet(axis_sizes, place, meanwhile):
    barrier = pltpu.get_barrier_semaphore()
    total = 0
    for axis, size in axis_sizes:
        for d in range(1, size):
            pl.semaphore_signal(barrier, inc=1, device_id=place(axis, d), device_id_type=MESH)
        total += size - 1
    meanwhile()
    pl.semaphore_wait(barrier, total)


def neighbour(n_grp, n_pts):
    group, col = lax.axis_index("grp"), lax.axis_index("pts")

    def place(axis, d):
        if axis == "grp":
            return (lax.rem(group + d, n_grp), col)
        return (group, lax.rem(col + d, n_pts))

    return place


def unit_inverse(a_ref, m_ref):
    sub = lax.broadcasted_iota(jnp.int32, (8, BLOCK), 0)
    m_ref[...] = (
        lax.broadcasted_iota(jnp.int32, (BLOCK, BLOCK), 0)
        == lax.broadcasted_iota(jnp.int32, (BLOCK, BLOCK), 1)
    ).astype(F32)

    def row(x, k):
        return jnp.broadcast_to(x[k : k + 1, :], (8, BLOCK))

    for b in range(BLOCK // 8):
        low = 8 * b
        pa = a_ref[low : low + 8, :]
        pm = m_ref[low : low + 8, :]
        cols = [jnp.broadcast_to(pa[:, low + j : low + j + 1], (8, BLOCK)) for j in range(8)]
        pivots = jnp.ones((8, BLOCK), F32)
        inverses = pivots
        for k in range(8):
            pivot = row(cols[k], k)
            inverse = 1.0 / pivot
            pivots = jnp.where(sub == k, pivot, pivots)
            inverses = jnp.where(sub == k, inverse, inverses)
            if k < 7:
                f = jnp.where(sub > k, cols[k] * inverse, 0.0)
                for j in range(k + 1, 8):
                    cols[j] = cols[j] - f * row(cols[j], k)
                pa = pa - f * row(pa, k)
                pm = pm - f * row(pm, k)
        if b < BLOCK // 8 - 1:
            below = pa.T[low + 8 :, :]
            a_ref[low + 8 :, :] -= dot(below, pa * inverses, HIGHEST)
            m_ref[low + 8 :, :] -= dot(below, pm * inverses, HIGHEST)
        scale = lax.rsqrt(pivots)
        scale = scale * (1.5 - 0.5 * pivots * scale * scale)
        m_ref[low : low + 8, :] = pm * scale


def prepare(blocks, weights_ref, schur, work, inv):
    wide = blocks.astype(F32)
    sq_high, sq_low = halves(wide * wide)
    ones = jnp.ones((EMBED, BLOCK), BF16)
    sq_col = dot(sq_high, ones) + dot(sq_low, ones)
    row_ones = jnp.ones((8, EMBED), BF16)
    sq_row = (dot_nt(row_ones, sq_high) + dot_nt(row_ones, sq_low))[0:1, :]
    weights_ref[2 * FACTOR :, :] = (2.0 * wide).T.astype(BF16)
    eye = (
        lax.broadcasted_iota(jnp.int32, (BLOCK, BLOCK), 0)
        == lax.broadcasted_iota(jnp.int32, (BLOCK, BLOCK), 1)
    )
    def span(i):
        return slice(i * BLOCK, (i + 1) * BLOCK)

    for i in range(ROUNDS):
        for j in range(i + 1):
            inner = dot_nt(blocks[span(i)], blocks[span(j)])
            dist = 2.0 * inner - sq_col[span(i)] - sq_row[:, span(j)]
            part = jnp.exp2(EXP_SCALE * dist)
            if i == j:
                part = part + jnp.where(eye, JITTER, 0.0)
            schur[i, j] = part

    for r in range(ROUNDS):
        work[...] = schur[r, r]
        unit_inverse(work, inv.at[r, r])
        for i in range(r + 1, ROUNDS):
            schur[i, r] = dot_nt(schur[i, r], inv[r, r], HIGHEST)
        for i in range(r + 1, ROUNDS):
            for j in range(r + 1, i + 1):
                schur[i, j] -= dot_nt(schur[i, r], schur[j, r], HIGHEST)

    inv[1, 0] = -dot(inv[1, 1], dot(schur[1, 0], inv[0, 0], HIGHEST), HIGHEST)
    inv[2, 1] = -dot(inv[2, 2], dot(schur[2, 1], inv[1, 1], HIGHEST), HIGHEST)
    inv[2, 0] = -dot(
        inv[2, 2],
        dot(schur[2, 0], inv[0, 0], HIGHEST) + dot(schur[2, 1], inv[1, 0], HIGHEST),
        HIGHEST,
    )
    for i in range(ROUNDS):
        for j in range(ROUNDS):
            if j <= i:
                high, low = halves(inv[i, j].T)
            else:
                high = low = jnp.zeros((BLOCK, BLOCK), BF16)
            weights_ref[span(j), span(i)] = high
            weights_ref[span(ROUNDS + j), span(i)] = low


def segment(counts, col, group, h, start, n_grp):
    odd = start & (n_grp - 1)
    begin = lax.div(start, n_grp) + jnp.where(group < odd, 1, 0)
    first = (group - odd) & (n_grp - 1)
    number = jnp.maximum(lax.div(counts[col, h] - first + n_grp - 1, n_grp), 0)
    return begin, number


def set_up(n_grp, n_pts, counts, owner, slot_ref, weights_ref, spots, shift_ref, doubled):
    group, col = lax.axis_index("grp"), lax.axis_index("pts")
    for r in range(ROUNDS):
        own_group, own_col = lax.div(owner[r], n_pts), lax.rem(owner[r], n_pts)
        begin = jnp.int32(0)
        for h in range(n_grp):
            begin += jnp.where(h < own_group, counts[own_col, h], 0)
        rank = begin + slot_ref[r : r + 1, :]
        here = (own_col == col) & ((rank & (n_grp - 1)) == group)
        spots[0:1, r * BLOCK : (r + 1) * BLOCK] = jnp.where(
            here, rank >> (n_grp.bit_length() - 1), -1
        )
    corner = weights_ref[2 * BLOCK : FACTOR, 2 * BLOCK :]
    doubled[0:BLOCK, :] = corner
    doubled[BLOCK:, :] = corner
    twice = weights_ref[2 * FACTOR :, :].astype(F32)
    high, low = halves(twice * twice)
    ones = jnp.ones((8, EMBED), BF16)
    shift_ref[...] = (-0.25 * EXP_SCALE) * (dot(ones, high) + dot(ones, low))[0:1, :]


def factor_rows(wide, base, weights_ref, spots, shift_ref, doubled):
    rows = wide.shape[0]
    high_ref, low_ref = weights_ref.at[0:FACTOR], weights_ref.at[FACTOR : 2 * FACTOR]
    twice_ref = weights_ref.at[2 * FACTOR :]
    x = wide.astype(BF16)
    sq = jnp.concatenate(halves(wide * wide), axis=1)
    sq = dot(sq, jnp.ones((2 * EMBED, BLOCK), BF16))
    spot = lax.broadcasted_iota(jnp.int32, (rows, BLOCK), 0) + base
    inner = dot(x, twice_ref[...])
    high, low = [], []
    for r in range(ROUNDS):
        at = slice(r * BLOCK, (r + 1) * BLOCK)
        part = jnp.exp2(EXP_SCALE * (inner[:, at] - sq) + shift_ref[0:1, at])
        part = part + jnp.where(spot == spots[0:1, at], JITTER, 0.0)
        a, b = halves(part)
        high.append(a)
        low.append(b)
    both = 2 * BLOCK
    high01 = jnp.concatenate(high[:2], axis=1)
    low01 = jnp.concatenate(low[:2], axis=1)
    first = (
        dot(high01, high_ref[0:both, :])
        + dot(low01, high_ref[0:both, :])
        + dot(high01, low_ref[0:both, :])
    )
    last = (
        dot(jnp.concatenate([high[2], low[2]], axis=1), doubled[...])
        + dot(high[2], low_ref[both:, both:])
    )
    parts = [first[:, 0:BLOCK], first[:, BLOCK:both], first[:, both:] + last]
    square = parts[0] * parts[0] + parts[1] * parts[1] + parts[2] * parts[2]
    square = jnp.concatenate(halves(square), axis=1)
    gain = (1.0 + JITTER) - dot_nt(jnp.ones((8, 2 * BLOCK), BF16), square)[0:1, :]
    return [p.astype(BF16) for p in parts], gain


def tabulate(counts, begins, numbers, n_grp):
    group, col = lax.axis_index("grp"), lax.axis_index("pts")
    start = jnp.int32(0)
    for h in range(n_grp):
        begin, number = segment(counts, col, group, h, start, n_grp)
        begins[h] = begin
        numbers[h] = number
        start += counts[col, h]


def first_source(begins, numbers, base, n_grp):
    source = jnp.int32(0)
    for h in range(n_grp):
        source += jnp.where(begins[h] + numbers[h] <= base, 1, 0)
    return jnp.minimum(source, n_grp - 1)


def exchange_kernel(
    n_grp, n_pts, counts, owner, slot_ref, patches_ref, got_ref, weights_ref, early_ref, gain_ref,
    spread_out, local, staged, points, begins, numbers, spots, shift_ref, doubled, local_sem, out_sems,
    x_ref, send_ref, order, picks_ref, got1, got2, part, gathered, schur, work, inv,
    load_sems, own_sem, *sems,
):
    group, col = lax.axis_index("grp"), lax.axis_index("pts")
    me = group * n_pts + col
    place = neighbour(n_grp, n_pts)
    (s1, r1), (s2, r2), (s3, r3) = sems[0:2], sems[2:4], sems[4:6]
    bulk = sems[6:]
    per_peer = send_ref.shape[1]
    edges = (0, FIRST_ROWS, EARLY_ROWS, per_peer)
    tile = order.shape[0]
    each = tile // n_grp
    loads = load_sems.shape[0]
    load_rows = x_ref.shape[0] // loads
    far_first = sorted(range(1, n_grp), key=lambda d: -min(d, n_grp - d))

    def load(i):
        span = pl.ds(i * load_rows, load_rows)
        return pltpu.make_async_copy(patches_ref.at[0, 0, span], x_ref.at[span], load_sems.at[i])

    for i in range(loads):
        load(i).start()

    def set_order():
        start = jnp.int32(0)
        for h in range(n_grp):
            start += jnp.where(h < group, counts[col, h], 0)
        to = lax.broadcasted_iota(jnp.int32, (tile, tile), 0)
        source = (to & (each - 1)) * n_grp + (((to >> (each.bit_length() - 1)) - start) & (n_grp - 1))
        hit = source == lax.broadcasted_iota(jnp.int32, (tile, tile), 1)
        order[...] = hit.astype(F32).astype(BF16)

    def sort_rows(low, high):
        for c in range(low // each, high // each):
            moved = dot(order[...], x_ref[c * tile : (c + 1) * tile, :]).astype(BF16)
            send_ref[:, c * each : (c + 1) * each, :] = moved.reshape(n_grp, each, EMBED)

    def find_picks():
        slots = jnp.full((1, BLOCK), -1, jnp.int32)
        for r in range(ROUNDS):
            slots = jnp.where(owner[r] == me, slot_ref[r : r + 1, :], slots)
        wanted = jnp.broadcast_to(slots, (BLOCK, BLOCK)).T
        wanted -= lax.broadcasted_iota(jnp.int32, (BLOCK, BLOCK), 1)
        unroll = 8

        def look(i, acc):
            for u in range(unroll):
                at = pl.multiple_of((i * unroll + u) * BLOCK, BLOCK)
                hit = (wanted == at).astype(F32).astype(BF16)
                acc += dot(hit, x_ref[pl.ds(at, BLOCK), :])
            return acc

        found = lax.fori_loop(
            0, x_ref.shape[0] // (unroll * BLOCK), look, jnp.zeros((BLOCK, EMBED), F32)
        )
        for r in range(ROUNDS):
            mine = jnp.where(owner[r] == me, found, 0.0).astype(BF16)
            per_round = BLOCK // PART_ROWS
            picks_ref[r * per_round : (r + 1) * per_round] = mine.reshape(per_round, PART_ROWS, EMBED)

    def rows(piece, d):
        span = pl.ds(edges[piece], edges[piece + 1] - edges[piece])
        target = lax.rem(group + d, n_grp)
        return pltpu.make_async_remote_copy(
            src_ref=send_ref.at[target, span],
            dst_ref=got_ref.at[group, span],
            send_sem=bulk[2 * piece].at[d],
            recv_sem=bulk[2 * piece + 1].at[d],
            device_id=place("grp", d),
            device_id_type=MESH,
        )

    def before():
        set_order()
        for i in range(FIRST_ROWS * n_grp // load_rows):
            load(i).wait()
        sort_rows(0, FIRST_ROWS)

    greet((("pts", n_pts), ("grp", n_grp)), place, before)
    for d in far_first:
        rows(0, d).start()
    for i in range(FIRST_ROWS * n_grp // load_rows, loads):
        load(i).wait()
    find_picks()

    def scatter(d):
        target = lax.rem(col + d, n_pts)
        return target, pltpu.make_async_remote_copy(
            src_ref=picks_ref.at[jnp.minimum(target, PARTS - 1)],
            dst_ref=got1.at[d - 1],
            send_sem=s1.at[d],
            recv_sem=r1.at[d],
            device_id=place("pts", d),
            device_id_type=MESH,
        )

    def across(d):
        return pltpu.make_async_remote_copy(
            src_ref=part.at[0],
            dst_ref=got2.at[d - 1],
            send_sem=s2.at[d],
            recv_sem=r2.at[d],
            device_id=place("grp", d),
            device_id_type=MESH,
        )

    def gather(d, owner):
        return pltpu.make_async_remote_copy(
            src_ref=part.at[1],
            dst_ref=gathered.at[owner],
            send_sem=s3.at[d],
            recv_sem=r3.at[d],
            device_id=place("pts", d),
            device_id_type=MESH,
        )

    for d in range(1, n_pts):
        target, copy = scatter(d)

        @pl.when(target < PARTS)
        def _():
            copy.start()

    sort_rows(FIRST_ROWS, per_peer)
    own = pltpu.make_async_copy(send_ref.at[group], got_ref.at[group], own_sem)
    own.start()

    @pl.when(col < PARTS)
    def _():
        acc = picks_ref[jnp.minimum(col, PARTS - 1)].astype(F32)
        for d in range(1, n_pts):
            scatter(d)[1].wait_recv()
            acc += got1[d - 1].astype(F32)
        part[0] = acc.astype(BF16)
        for d in range(1, n_grp):
            across(d).start()

    for piece in (1, 2):
        for d in far_first:
            rows(piece, d).start()

    @pl.when(col < PARTS)
    def _():
        acc = part[0].astype(F32)
        for d in range(1, n_grp):
            across(d).wait_recv()
            acc += got2[d - 1].astype(F32)
        part[1] = acc.astype(BF16)
        for d in range(1, n_pts):
            gather(d, col).start()
        gathered[col] = part[1]

    for d in range(1, n_pts):
        source = lax.rem(col + n_pts - d, n_pts)

        @pl.when(source < PARTS)
        def _():
            gather(d, source).wait_recv()

    prepare(gathered[...].reshape(FACTOR, EMBED), weights_ref, schur, work, inv)
    set_up(n_grp, n_pts, counts, owner, slot_ref, weights_ref, spots, shift_ref, doubled)
    tabulate(counts, begins, numbers, n_grp)
    spread_out[:, 0:BLOCK, :] = jnp.zeros((n_grp, BLOCK, EMBED), F32)
    spread_out[:, BLOCK + EARLY_ROWS :, :] = jnp.zeros((n_grp, BLOCK, EMBED), F32)

    own.wait()
    for piece in (0, 1):
        for d in far_first:
            rows(piece, d).wait_recv()
    fetch = pltpu.make_async_copy(got_ref.at[:, pl.ds(0, EARLY_ROWS)], local, local_sem)
    fetch.start()
    fetch.wait()

    def widen(h, _):
        spread_out[h, BLOCK : BLOCK + EARLY_ROWS, :] = local[h].astype(F32)
        return 0

    lax.fori_loop(0, n_grp, widen, 0)
    row = lax.broadcasted_iota(jnp.int32, (BLOCK, EMBED), 0)
    step_rows = points.shape[0]

    per_step = step_rows // BLOCK

    def out_copy(i):
        span = pl.ds(i * per_step, per_step)
        return pltpu.make_async_copy(staged.at[span], early_ref.at[span], out_sems.at[i])

    def early(i, _):
        base = pl.multiple_of(i * step_rows, step_rows)
        for b in range(step_rows // BLOCK):
            first = first_source(begins, numbers, base + b * BLOCK, n_grp)
            x = jnp.zeros((BLOCK, EMBED), F32)
            for k in range(SOURCES):
                source = jnp.minimum(first + k, n_grp - 1)
                skip = base + b * BLOCK - begins[source]
                limit = jnp.minimum(numbers[source], EARLY_ROWS)
                at = jnp.clip(skip, -BLOCK, EARLY_ROWS) + BLOCK
                new = spread_out[source, pl.ds(at, BLOCK), :]
                x = jnp.where((row + skip >= 0) & (row + skip < limit), new, x)
            points[b * BLOCK : (b + 1) * BLOCK, :] = x
        parts, gain = factor_rows(points[...], base, weights_ref, spots, shift_ref, doubled)
        for b in range(per_step):
            for r in range(ROUNDS):
                staged[i * per_step + b, :, r * BLOCK : (r + 1) * BLOCK] = parts[r][
                    b * BLOCK : (b + 1) * BLOCK, :
                ]
            gain_ref[pl.ds(i * (step_rows // BLOCK) + b, 1), :] = gain[:, b * BLOCK : (b + 1) * BLOCK]
        out_copy(i).start()
        return 0

    lax.fori_loop(0, out_sems.shape[0], early, 0)

    for d in range(1, n_pts):
        target, copy = scatter(d)

        @pl.when(target < PARTS)
        def _():
            copy.wait_send()

    @pl.when(col < PARTS)
    def _():
        for d in range(1, n_grp):
            across(d).wait_send()
        for d in range(1, n_pts):
            gather(d, col).wait_send()

    def finish(i, _):
        out_copy(i).wait()
        return 0

    lax.fori_loop(0, out_sems.shape[0], finish, 0)
    for d in far_first:
        rows(2, d).wait_recv()
    for piece in range(3):
        for d in far_first:
            rows(piece, d).wait_send()


def exchange(patches, counts, pick_slot, block_owner, n_grp, n_pts):
    slots = patches.shape[2]
    shape = (PARTS, PART_ROWS, EMBED)
    square = (ROUNDS, ROUNDS, BLOCK, BLOCK)
    messages = (n_grp, slots // n_grp, EMBED)
    points = slots // 2
    rows = 512
    return pl.pallas_call(
        functools.partial(exchange_kernel, n_grp, n_pts),
        out_shape=(
            jax.ShapeDtypeStruct(messages, BF16),
            jax.ShapeDtypeStruct((2 * FACTOR + EMBED, FACTOR), BF16),
            jax.ShapeDtypeStruct((points // BLOCK, BLOCK, FACTOR), BF16),
            jax.ShapeDtypeStruct((points // BLOCK, BLOCK), F32),
        ),
        in_specs=[
            pl.BlockSpec(memory_space=pltpu.SMEM),
            pl.BlockSpec(memory_space=pltpu.SMEM),
            pl.BlockSpec(memory_space=pltpu.VMEM),
            pl.BlockSpec(memory_space=pltpu.HBM),
        ],
        out_specs=(
            pl.BlockSpec(memory_space=pltpu.HBM),
            pl.BlockSpec(memory_space=pltpu.VMEM),
            pl.BlockSpec(memory_space=pltpu.HBM),
            pl.BlockSpec(memory_space=pltpu.VMEM),
        ),
        scratch_shapes=[
            pltpu.VMEM((n_grp, EARLY_ROWS + 2 * BLOCK, EMBED), F32),
            pltpu.VMEM((n_grp, EARLY_ROWS, EMBED), BF16),
            pltpu.VMEM((points // BLOCK, BLOCK, FACTOR), BF16),
            pltpu.VMEM((rows, EMBED), F32),
            pltpu.SMEM((n_grp,), jnp.int32),
            pltpu.SMEM((n_grp,), jnp.int32),
            pltpu.VMEM((1, FACTOR), jnp.int32),
            pltpu.VMEM((1, FACTOR), F32),
            pltpu.VMEM((2 * BLOCK, BLOCK), BF16),
            pltpu.SemaphoreType.DMA,
            pltpu.SemaphoreType.DMA((points // rows,)),
            pltpu.VMEM((slots, EMBED), BF16),
            pltpu.VMEM(messages, BF16),
            pltpu.VMEM((n_grp * 16, n_grp * 16), BF16),
            pltpu.VMEM(shape, BF16),
            pltpu.VMEM((n_pts - 1,) + shape[1:], BF16),
            pltpu.VMEM((n_grp - 1,) + shape[1:], BF16),
            pltpu.VMEM((2,) + shape[1:], BF16),
            pltpu.VMEM(shape, BF16),
            pltpu.VMEM(square, F32),
            pltpu.VMEM((BLOCK, BLOCK), F32),
            pltpu.VMEM(square, F32),
            pltpu.SemaphoreType.DMA((8,)),
            pltpu.SemaphoreType.DMA,
        ]
        + [pltpu.SemaphoreType.DMA((n,)) for n in (n_pts, n_pts, n_grp, n_grp, n_pts, n_pts)]
        + [pltpu.SemaphoreType.DMA((n_grp,))] * 6,
        compiler_params=pltpu.CompilerParams(
            collective_id=0, has_side_effects=True, vmem_limit_bytes=58 << 20
        ),
        name="exchange",
    )(counts, block_owner, pick_slot, patches)


def late_kernel(
    n_grp, n_pts, counts, owner, slot_ref, got_in, weights_ref, gain_in, early_ref,
    out_ref, gain_ref, got_ref, window, staged, begins, numbers, flags, spots, shift_ref, doubled, in_sems, sems,
):
    in_early = pltpu.make_async_copy(early_ref, staged, in_sems.at[0])
    in_early.start()
    in_got = pltpu.make_async_copy(got_in, got_ref, in_sems.at[1])
    in_got.start()
    per_peer = got_ref.shape[1]
    n_blocks = gain_ref.shape[0]
    reach = BLOCK + 16
    gain_ref[...] = gain_in[...]
    tabulate(counts, begins, numbers, n_grp)
    for b in range(n_blocks):
        flags[b] = 0
    for h in range(n_grp):
        end = begins[h] + numbers[h]

        def mark(b, _):
            flags[b] = 1
            return 0

        low = lax.div(begins[h] + EARLY_ROWS, BLOCK)
        high = jnp.where(numbers[h] > EARLY_ROWS, lax.div(end - 1, BLOCK) + 1, low)
        lax.fori_loop(low, high, mark, 0)
        if h + SOURCES < n_grp:
            last = lax.div(jnp.maximum(end - 1, 0), BLOCK)

            @pl.when(last == lax.div(begins[h + SOURCES], BLOCK))
            def _():
                flags[last] = 1

    def span(b):
        return pl.ds(pl.multiple_of(b * BLOCK, BLOCK), BLOCK)

    def copy_new(b):
        return pltpu.make_async_copy(staged.at[b], out_ref.at[0, 0, span(b), :], sems.at[b])

    def keep(b, _):
        @pl.when(flags[b] == 0)
        def _():
            copy_new(b).start()

        return 0

    set_up(n_grp, n_pts, counts, owner, slot_ref, weights_ref, spots, shift_ref, doubled)
    window[...] = jnp.zeros_like(window)
    in_early.wait()
    lax.fori_loop(0, n_blocks, keep, 0)
    in_got.wait()
    row = lax.broadcasted_iota(jnp.int32, (BLOCK, EMBED), 0)

    def redo(b, _):
        @pl.when(flags[b] == 1)
        def _():
            base = pl.multiple_of(b * BLOCK, BLOCK)
            first = first_source(begins, numbers, base, n_grp)
            stop = jnp.int32(0)
            for h in range(n_grp):
                stop += jnp.where(begins[h] < base + BLOCK, 1, 0)

            def add(source, x):
                skip = base - begins[source]
                at = jnp.clip((skip >> 4) << 4, 0, per_peer - reach)
                at = pl.multiple_of(at, 16)
                window[BLOCK : BLOCK + reach, :] = got_ref[source, pl.ds(at, reach), :].astype(F32)
                begin = jnp.clip(skip - at, -BLOCK, reach) + BLOCK
                new = window[pl.ds(begin, BLOCK), :]
                return jnp.where((row + skip >= 0) & (row + skip < numbers[source]), new, x)

            x = lax.fori_loop(first, stop, add, jnp.zeros((BLOCK, EMBED), F32))
            parts, gain = factor_rows(x, base, weights_ref, spots, shift_ref, doubled)
            for r in range(ROUNDS):
                staged[b, :, r * BLOCK : (r + 1) * BLOCK] = parts[r]
            gain_ref[pl.ds(b, 1), :] = gain
            copy_new(b).start()

        return 0

    lax.fori_loop(0, n_blocks, redo, 0)

    def finish(b, _):
        copy_new(b).wait()
        return 0

    lax.fori_loop(0, n_blocks, finish, 0)


def late(got, counts, pick_slot, block_owner, weights, gain, early_rows, n_grp, n_pts):
    n_blocks = gain.shape[0]
    smem = pl.BlockSpec(memory_space=pltpu.SMEM)
    vmem = pl.BlockSpec(memory_space=pltpu.VMEM)
    hbm = pl.BlockSpec(memory_space=pltpu.HBM)
    return pl.pallas_call(
        functools.partial(late_kernel, n_grp, n_pts),
        out_shape=(
            jax.ShapeDtypeStruct((1, 1, n_blocks * BLOCK, FACTOR), BF16),
            jax.ShapeDtypeStruct(gain.shape, F32),
        ),
        in_specs=[smem, smem, vmem, hbm, vmem, vmem, hbm],
        out_specs=(hbm, vmem),
        scratch_shapes=[
            pltpu.VMEM(got.shape, BF16),
            pltpu.VMEM((3 * BLOCK + 16, EMBED), F32),
            pltpu.VMEM((n_blocks, BLOCK, FACTOR), BF16),
            pltpu.SMEM((n_grp,), jnp.int32),
            pltpu.SMEM((n_grp,), jnp.int32),
            pltpu.SMEM((n_blocks,), jnp.int32),
            pltpu.VMEM((1, FACTOR), jnp.int32),
            pltpu.VMEM((1, FACTOR), F32),
            pltpu.VMEM((2 * BLOCK, BLOCK), BF16),
            pltpu.SemaphoreType.DMA((2,)),
            pltpu.SemaphoreType.DMA((n_blocks,)),
        ],
        compiler_params=pltpu.CompilerParams(vmem_limit_bytes=58 << 20),
        name="late",
    )(counts, block_owner, pick_slot, got, weights, gain, early_rows)


def per_device(patches, counts, pick_slot, block_owner):
    n_grp, n_pts = lax.axis_size("grp"), lax.axis_size("pts")
    got, weights, rows, gain = exchange(patches, counts, pick_slot, block_owner, n_grp, n_pts)
    rows, gain = late(got, counts, pick_slot, block_owner, weights, gain, rows, n_grp, n_pts)
    return rows, gain.reshape(1, 1, gain.size)


def solution(mesh):
    in_specs = (P("grp", "pts", None, None), P(), P(), P())
    out_specs = (P("grp", "pts", None, None), P("grp", "pts", None))
    return jax.shard_map(
        per_device, mesh=mesh, in_specs=in_specs, out_specs=out_specs, check_vma=False
    )
```

```python
import functools
import math

import jax
import jax.numpy as jnp
from jax import lax
from jax.experimental import pallas as pl
from jax.experimental.pallas import tpu as pltpu
from jax.sharding import PartitionSpec as P

MESH = pl.DeviceIdType.MESH
HIGHEST = lax.Precision.HIGHEST
JITTER = 0.1
EMBED = 128
BLOCK = 128
ROUNDS = 3
FACTOR = ROUNDS * BLOCK
PARTS = 12
PART_ROWS = FACTOR // PARTS
FIRST_ROWS = 256
EARLY_ROWS = 768
SOURCES = 3
EXP_SCALE = math.log2(math.e) / EMBED
F32 = jnp.float32
BF16 = jnp.bfloat16


def dot(a, b, precision=None):
    return jnp.dot(a, b, precision=precision, preferred_element_type=F32)


def dot_nt(a, b, precision=None):
    return lax.dot_general(
        a, b, (((1,), (1,)), ((), ())), precision=precision, preferred_element_type=F32
    )


def halves(x):
    high = x.astype(BF16)
    return high, (x - high.astype(F32)).astype(BF16)


def greet(axis_sizes, place, meanwhile):
    barrier = pltpu.get_barrier_semaphore()
    total = 0
    for axis, size in axis_sizes:
        for d in range(1, size):
            pl.semaphore_signal(barrier, inc=1, device_id=place(axis, d), device_id_type=MESH)
        total += size - 1
    meanwhile()
    pl.semaphore_wait(barrier, total)


def neighbour(n_grp, n_pts):
    group, col = lax.axis_index("grp"), lax.axis_index("pts")

    def place(axis, d):
        if axis == "grp":
            return (lax.rem(group + d, n_grp), col)
        return (group, lax.rem(col + d, n_pts))

    return place


def unit_inverse(a_ref, m_ref):
    sub = lax.broadcasted_iota(jnp.int32, (8, BLOCK), 0)
    m_ref[...] = (
        lax.broadcasted_iota(jnp.int32, (BLOCK, BLOCK), 0)
        == lax.broadcasted_iota(jnp.int32, (BLOCK, BLOCK), 1)
    ).astype(F32)

    def row(x, k):
        return jnp.broadcast_to(x[k : k + 1, :], (8, BLOCK))

    for b in range(BLOCK // 8):
        low = 8 * b
        pa = a_ref[low : low + 8, :]
        pm = m_ref[low : low + 8, :]
        cols = [jnp.broadcast_to(pa[:, low + j : low + j + 1], (8, BLOCK)) for j in range(8)]
        pivots = jnp.ones((8, BLOCK), F32)
        inverses = pivots
        for k in range(8):
            pivot = row(cols[k], k)
            inverse = 1.0 / pivot
            pivots = jnp.where(sub == k, pivot, pivots)
            inverses = jnp.where(sub == k, inverse, inverses)
            if k < 7:
                f = jnp.where(sub > k, cols[k] * inverse, 0.0)
                for j in range(k + 1, 8):
                    cols[j] = cols[j] - f * row(cols[j], k)
                pa = pa - f * row(pa, k)
                pm = pm - f * row(pm, k)
        if b < BLOCK // 8 - 1:
            below = pa.T[low + 8 :, :]
            a_ref[low + 8 :, :] -= dot(below, pa * inverses, HIGHEST)
            m_ref[low + 8 :, :] -= dot(below, pm * inverses, HIGHEST)
        scale = lax.rsqrt(pivots)
        scale = scale * (1.5 - 0.5 * pivots * scale * scale)
        m_ref[low : low + 8, :] = pm * scale


def prepare(blocks, weights_ref, schur, work, inv):
    wide = blocks.astype(F32)
    sq_high, sq_low = halves(wide * wide)
    ones = jnp.ones((EMBED, BLOCK), BF16)
    sq_col = dot(sq_high, ones) + dot(sq_low, ones)
    row_ones = jnp.ones((8, EMBED), BF16)
    sq_row = (dot_nt(row_ones, sq_high) + dot_nt(row_ones, sq_low))[0:1, :]
    weights_ref[2 * FACTOR :, :] = (2.0 * wide).T.astype(BF16)
    eye = (
        lax.broadcasted_iota(jnp.int32, (BLOCK, BLOCK), 0)
        == lax.broadcasted_iota(jnp.int32, (BLOCK, BLOCK), 1)
    )
    def span(i):
        return slice(i * BLOCK, (i + 1) * BLOCK)

    for i in range(ROUNDS):
        for j in range(i + 1):
            inner = dot_nt(blocks[span(i)], blocks[span(j)])
            dist = 2.0 * inner - sq_col[span(i)] - sq_row[:, span(j)]
            part = jnp.exp2(EXP_SCALE * dist)
            if i == j:
                part = part + jnp.where(eye, JITTER, 0.0)
            schur[i, j] = part

    for r in range(ROUNDS):
        work[...] = schur[r, r]
        unit_inverse(work, inv.at[r, r])
        for i in range(r + 1, ROUNDS):
            schur[i, r] = dot_nt(schur[i, r], inv[r, r], HIGHEST)
        for i in range(r + 1, ROUNDS):
            for j in range(r + 1, i + 1):
                schur[i, j] -= dot_nt(schur[i, r], schur[j, r], HIGHEST)

    inv[1, 0] = -dot(inv[1, 1], dot(schur[1, 0], inv[0, 0], HIGHEST), HIGHEST)
    inv[2, 1] = -dot(inv[2, 2], dot(schur[2, 1], inv[1, 1], HIGHEST), HIGHEST)
    inv[2, 0] = -dot(
        inv[2, 2],
        dot(schur[2, 0], inv[0, 0], HIGHEST) + dot(schur[2, 1], inv[1, 0], HIGHEST),
        HIGHEST,
    )
    for i in range(ROUNDS):
        for j in range(ROUNDS):
            if j <= i:
                high, low = halves(inv[i, j].T)
            else:
                high = low = jnp.zeros((BLOCK, BLOCK), BF16)
            weights_ref[span(j), span(i)] = high
            weights_ref[span(ROUNDS + j), span(i)] = low


def segment(counts, col, group, h, start, n_grp):
    odd = start & (n_grp - 1)
    begin = lax.div(start, n_grp) + jnp.where(group < odd, 1, 0)
    first = (group - odd) & (n_grp - 1)
    number = jnp.maximum(lax.div(counts[col, h] - first + n_grp - 1, n_grp), 0)
    return begin, number


def set_up(n_grp, n_pts, counts, owner, slot_ref, weights_ref, spots, shift_ref, doubled):
    group, col = lax.axis_index("grp"), lax.axis_index("pts")
    for r in range(ROUNDS):
        own_group, own_col = lax.div(owner[r], n_pts), lax.rem(owner[r], n_pts)
        begin = jnp.int32(0)
        for h in range(n_grp):
            begin += jnp.where(h < own_group, counts[own_col, h], 0)
        rank = begin + slot_ref[r : r + 1, :]
        here = (own_col == col) & ((rank & (n_grp - 1)) == group)
        spots[0:1, r * BLOCK : (r + 1) * BLOCK] = jnp.where(
            here, rank >> (n_grp.bit_length() - 1), -1
        )
    corner = weights_ref[2 * BLOCK : FACTOR, 2 * BLOCK :]
    doubled[0:BLOCK, :] = corner
    doubled[BLOCK:, :] = corner
    twice = weights_ref[2 * FACTOR :, :].astype(F32)
    high, low = halves(twice * twice)
    ones = jnp.ones((8, EMBED), BF16)
    shift_ref[...] = (-0.25 * EXP_SCALE) * (dot(ones, high) + dot(ones, low))[0:1, :]


def factor_rows(wide, base, weights_ref, spots, shift_ref, doubled):
    rows = wide.shape[0]
    high_ref, low_ref = weights_ref.at[0:FACTOR], weights_ref.at[FACTOR : 2 * FACTOR]
    twice_ref = weights_ref.at[2 * FACTOR :]
    x = wide.astype(BF16)
    sq = jnp.concatenate(halves(wide * wide), axis=1)
    sq = dot(sq, jnp.ones((2 * EMBED, BLOCK), BF16))
    spot = lax.broadcasted_iota(jnp.int32, (rows, BLOCK), 0) + base
    inner = dot(x, twice_ref[...])
    high, low = [], []
    for r in range(ROUNDS):
        at = slice(r * BLOCK, (r + 1) * BLOCK)
        part = jnp.exp2(EXP_SCALE * (inner[:, at] - sq) + shift_ref[0:1, at])
        part = part + jnp.where(spot == spots[0:1, at], JITTER, 0.0)
        a, b = halves(part)
        high.append(a)
        low.append(b)
    both = 2 * BLOCK
    high01 = jnp.concatenate(high[:2], axis=1)
    low01 = jnp.concatenate(low[:2], axis=1)
    first = (
        dot(high01, high_ref[0:both, :])
        + dot(low01, high_ref[0:both, :])
        + dot(high01, low_ref[0:both, :])
    )
    last = (
        dot(jnp.concatenate([high[2], low[2]], axis=1), doubled[...])
        + dot(high[2], low_ref[both:, both:])
    )
    parts = [first[:, 0:BLOCK], first[:, BLOCK:both], first[:, both:] + last]
    square = parts[0] * parts[0] + parts[1] * parts[1] + parts[2] * parts[2]
    square = jnp.concatenate(halves(square), axis=1)
    gain = (1.0 + JITTER) - dot_nt(jnp.ones((8, 2 * BLOCK), BF16), square)[0:1, :]
    return [p.astype(BF16) for p in parts], gain


def tabulate(counts, begins, numbers, n_grp):
    group, col = lax.axis_index("grp"), lax.axis_index("pts")
    start = jnp.int32(0)
    for h in range(n_grp):
        begin, number = segment(counts, col, group, h, start, n_grp)
        begins[h] = begin
        numbers[h] = number
        start += counts[col, h]


def first_source(begins, numbers, base, n_grp):
    source = jnp.int32(0)
    for h in range(n_grp):
        source += jnp.where(begins[h] + numbers[h] <= base, 1, 0)
    return jnp.minimum(source, n_grp - 1)


def exchange_kernel(
    n_grp, n_pts, counts, owner, slot_ref, patches_ref, got_ref, weights_ref, early_ref, gain_ref,
    spread_out, local, staged, points, begins, numbers, spots, shift_ref, doubled, local_sem, out_sems,
    x_ref, send_ref, order, picks_ref, got1, got2, part, gathered, schur, work, inv,
    load_sems, own_sem, *sems,
):
    group, col = lax.axis_index("grp"), lax.axis_index("pts")
    me = group * n_pts + col
    place = neighbour(n_grp, n_pts)
    (s1, r1), (s2, r2), (s3, r3) = sems[0:2], sems[2:4], sems[4:6]
    bulk = sems[6:]
    per_peer = send_ref.shape[1]
    edges = (0, FIRST_ROWS, EARLY_ROWS, per_peer)
    tile = order.shape[0]
    each = tile // n_grp
    loads = load_sems.shape[0]
    load_rows = x_ref.shape[0] // loads
    near_first = sorted(range(1, n_grp), key=lambda d: min(d, n_grp - d))

    def load(i):
        span = pl.ds(i * load_rows, load_rows)
        return pltpu.make_async_copy(patches_ref.at[0, 0, span], x_ref.at[span], load_sems.at[i])

    for i in range(loads):
        load(i).start()

    def set_order():
        start = jnp.int32(0)
        for h in range(n_grp):
            start += jnp.where(h < group, counts[col, h], 0)
        to = lax.broadcasted_iota(jnp.int32, (tile, tile), 0)
        source = (to & (each - 1)) * n_grp + (((to >> (each.bit_length() - 1)) - start) & (n_grp - 1))
        hit = source == lax.broadcasted_iota(jnp.int32, (tile, tile), 1)
        order[...] = hit.astype(F32).astype(BF16)

    def sort_rows(low, high):
        for c in range(low // each, high // each):
            moved = dot(order[...], x_ref[c * tile : (c + 1) * tile, :]).astype(BF16)
            send_ref[:, c * each : (c + 1) * each, :] = moved.reshape(n_grp, each, EMBED)

    def find_picks():
        slots = jnp.full((1, BLOCK), -1, jnp.int32)
        for r in range(ROUNDS):
            slots = jnp.where(owner[r] == me, slot_ref[r : r + 1, :], slots)
        wanted = jnp.broadcast_to(slots, (BLOCK, BLOCK)).T
        wanted -= lax.broadcasted_iota(jnp.int32, (BLOCK, BLOCK), 1)
        unroll = 8

        def look(i, acc):
            for u in range(unroll):
                at = pl.multiple_of((i * unroll + u) * BLOCK, BLOCK)
                hit = (wanted == at).astype(F32).astype(BF16)
                acc += dot(hit, x_ref[pl.ds(at, BLOCK), :])
            return acc

        found = lax.fori_loop(
            0, x_ref.shape[0] // (unroll * BLOCK), look, jnp.zeros((BLOCK, EMBED), F32)
        )
        for r in range(ROUNDS):
            mine = jnp.where(owner[r] == me, found, 0.0).astype(BF16)
            per_round = BLOCK // PART_ROWS
            picks_ref[r * per_round : (r + 1) * per_round] = mine.reshape(per_round, PART_ROWS, EMBED)

    def rows(piece, d):
        span = pl.ds(edges[piece], edges[piece + 1] - edges[piece])
        target = lax.rem(group + d, n_grp)
        return pltpu.make_async_remote_copy(
            src_ref=send_ref.at[target, span],
            dst_ref=got_ref.at[group, span],
            send_sem=bulk[2 * piece].at[d],
            recv_sem=bulk[2 * piece + 1].at[d],
            device_id=place("grp", d),
            device_id_type=MESH,
        )

    def before():
        set_order()
        for i in range(FIRST_ROWS * n_grp // load_rows):
            load(i).wait()
        sort_rows(0, FIRST_ROWS)

    greet((("pts", n_pts), ("grp", n_grp)), place, before)
    for d in near_first:
        rows(0, d).start()
    for i in range(FIRST_ROWS * n_grp // load_rows, loads):
        load(i).wait()
    find_picks()

    def scatter(d):
        target = lax.rem(col + d, n_pts)
        return target, pltpu.make_async_remote_copy(
            src_ref=picks_ref.at[jnp.minimum(target, PARTS - 1)],
            dst_ref=got1.at[d - 1],
            send_sem=s1.at[d],
            recv_sem=r1.at[d],
            device_id=place("pts", d),
            device_id_type=MESH,
        )

    def across(d):
        return pltpu.make_async_remote_copy(
            src_ref=part.at[0],
            dst_ref=got2.at[d - 1],
            send_sem=s2.at[d],
            recv_sem=r2.at[d],
            device_id=place("grp", d),
            device_id_type=MESH,
        )

    def gather(d, owner):
        return pltpu.make_async_remote_copy(
            src_ref=part.at[1],
            dst_ref=gathered.at[owner],
            send_sem=s3.at[d],
            recv_sem=r3.at[d],
            device_id=place("pts", d),
            device_id_type=MESH,
        )

    for d in range(1, n_pts):
        target, copy = scatter(d)

        @pl.when(target < PARTS)
        def _():
            copy.start()

    sort_rows(FIRST_ROWS, per_peer)
    own = pltpu.make_async_copy(send_ref.at[group], got_ref.at[group], own_sem)
    own.start()

    @pl.when(col < PARTS)
    def _():
        acc = picks_ref[jnp.minimum(col, PARTS - 1)].astype(F32)
        for d in range(1, n_pts):
            scatter(d)[1].wait_recv()
            acc += got1[d - 1].astype(F32)
        part[0] = acc.astype(BF16)
        for d in range(1, n_grp):
            across(d).start()

    for piece in (1, 2):
        for d in near_first:
            rows(piece, d).start()

    @pl.when(col < PARTS)
    def _():
        acc = part[0].astype(F32)
        for d in range(1, n_grp):
            across(d).wait_recv()
            acc += got2[d - 1].astype(F32)
        part[1] = acc.astype(BF16)
        for d in range(1, n_pts):
            gather(d, col).start()
        gathered[col] = part[1]

    for d in range(1, n_pts):
        source = lax.rem(col + n_pts - d, n_pts)

        @pl.when(source < PARTS)
        def _():
            gather(d, source).wait_recv()

    prepare(gathered[...].reshape(FACTOR, EMBED), weights_ref, schur, work, inv)
    set_up(n_grp, n_pts, counts, owner, slot_ref, weights_ref, spots, shift_ref, doubled)
    tabulate(counts, begins, numbers, n_grp)
    spread_out[:, 0:BLOCK, :] = jnp.zeros((n_grp, BLOCK, EMBED), F32)
    spread_out[:, BLOCK + EARLY_ROWS :, :] = jnp.zeros((n_grp, BLOCK, EMBED), F32)

    own.wait()
    for piece in (0, 1):
        for d in near_first:
            rows(piece, d).wait_recv()
    fetch = pltpu.make_async_copy(got_ref.at[:, pl.ds(0, EARLY_ROWS)], local, local_sem)
    fetch.start()
    fetch.wait()

    def widen(h, _):
        spread_out[h, BLOCK : BLOCK + EARLY_ROWS, :] = local[h].astype(F32)
        return 0

    lax.fori_loop(0, n_grp, widen, 0)
    row = lax.broadcasted_iota(jnp.int32, (BLOCK, EMBED), 0)
    step_rows = points.shape[0]

    per_step = step_rows // BLOCK

    def out_copy(i):
        span = pl.ds(i * per_step, per_step)
        return pltpu.make_async_copy(staged.at[span], early_ref.at[span], out_sems.at[i])

    def early(i, _):
        base = pl.multiple_of(i * step_rows, step_rows)
        for b in range(step_rows // BLOCK):
            first = first_source(begins, numbers, base + b * BLOCK, n_grp)
            x = jnp.zeros((BLOCK, EMBED), F32)
            for k in range(SOURCES):
                source = jnp.minimum(first + k, n_grp - 1)
                skip = base + b * BLOCK - begins[source]
                limit = jnp.minimum(numbers[source], EARLY_ROWS)
                at = jnp.clip(skip, -BLOCK, EARLY_ROWS) + BLOCK
                new = spread_out[source, pl.ds(at, BLOCK), :]
                x = jnp.where((row + skip >= 0) & (row + skip < limit), new, x)
            points[b * BLOCK : (b + 1) * BLOCK, :] = x
        parts, gain = factor_rows(points[...], base, weights_ref, spots, shift_ref, doubled)
        for b in range(per_step):
            for r in range(ROUNDS):
                staged[i * per_step + b, :, r * BLOCK : (r + 1) * BLOCK] = parts[r][
                    b * BLOCK : (b + 1) * BLOCK, :
                ]
            gain_ref[pl.ds(i * (step_rows // BLOCK) + b, 1), :] = gain[:, b * BLOCK : (b + 1) * BLOCK]
        out_copy(i).start()
        return 0

    lax.fori_loop(0, out_sems.shape[0], early, 0)

    for d in range(1, n_pts):
        target, copy = scatter(d)

        @pl.when(target < PARTS)
        def _():
            copy.wait_send()

    @pl.when(col < PARTS)
    def _():
        for d in range(1, n_grp):
            across(d).wait_send()
        for d in range(1, n_pts):
            gather(d, col).wait_send()

    def finish(i, _):
        out_copy(i).wait()
        return 0

    lax.fori_loop(0, out_sems.shape[0], finish, 0)
    for d in near_first:
        rows(2, d).wait_recv()
    for piece in range(3):
        for d in near_first:
            rows(piece, d).wait_send()


def exchange(patches, counts, pick_slot, block_owner, n_grp, n_pts):
    slots = patches.shape[2]
    shape = (PARTS, PART_ROWS, EMBED)
    square = (ROUNDS, ROUNDS, BLOCK, BLOCK)
    messages = (n_grp, slots // n_grp, EMBED)
    points = slots // 2
    rows = 512
    return pl.pallas_call(
        functools.partial(exchange_kernel, n_grp, n_pts),
        out_shape=(
            jax.ShapeDtypeStruct(messages, BF16),
            jax.ShapeDtypeStruct((2 * FACTOR + EMBED, FACTOR), BF16),
            jax.ShapeDtypeStruct((points // BLOCK, BLOCK, FACTOR), BF16),
            jax.ShapeDtypeStruct((points // BLOCK, BLOCK), F32),
        ),
        in_specs=[
            pl.BlockSpec(memory_space=pltpu.SMEM),
            pl.BlockSpec(memory_space=pltpu.SMEM),
            pl.BlockSpec(memory_space=pltpu.VMEM),
            pl.BlockSpec(memory_space=pltpu.HBM),
        ],
        out_specs=(
            pl.BlockSpec(memory_space=pltpu.HBM),
            pl.BlockSpec(memory_space=pltpu.VMEM),
            pl.BlockSpec(memory_space=pltpu.HBM),
            pl.BlockSpec(memory_space=pltpu.VMEM),
        ),
        scratch_shapes=[
            pltpu.VMEM((n_grp, EARLY_ROWS + 2 * BLOCK, EMBED), F32),
            pltpu.VMEM((n_grp, EARLY_ROWS, EMBED), BF16),
            pltpu.VMEM((points // BLOCK, BLOCK, FACTOR), BF16),
            pltpu.VMEM((rows, EMBED), F32),
            pltpu.SMEM((n_grp,), jnp.int32),
            pltpu.SMEM((n_grp,), jnp.int32),
            pltpu.VMEM((1, FACTOR), jnp.int32),
            pltpu.VMEM((1, FACTOR), F32),
            pltpu.VMEM((2 * BLOCK, BLOCK), BF16),
            pltpu.SemaphoreType.DMA,
            pltpu.SemaphoreType.DMA((points // rows,)),
            pltpu.VMEM((slots, EMBED), BF16),
            pltpu.VMEM(messages, BF16),
            pltpu.VMEM((n_grp * 16, n_grp * 16), BF16),
            pltpu.VMEM(shape, BF16),
            pltpu.VMEM((n_pts - 1,) + shape[1:], BF16),
            pltpu.VMEM((n_grp - 1,) + shape[1:], BF16),
            pltpu.VMEM((2,) + shape[1:], BF16),
            pltpu.VMEM(shape, BF16),
            pltpu.VMEM(square, F32),
            pltpu.VMEM((BLOCK, BLOCK), F32),
            pltpu.VMEM(square, F32),
            pltpu.SemaphoreType.DMA((8,)),
            pltpu.SemaphoreType.DMA,
        ]
        + [pltpu.SemaphoreType.DMA((n,)) for n in (n_pts, n_pts, n_grp, n_grp, n_pts, n_pts)]
        + [pltpu.SemaphoreType.DMA((n_grp,))] * 6,
        compiler_params=pltpu.CompilerParams(
            collective_id=0, has_side_effects=True, vmem_limit_bytes=58 << 20
        ),
        name="exchange",
    )(counts, block_owner, pick_slot, patches)


def late_kernel(
    n_grp, n_pts, counts, owner, slot_ref, got_in, weights_ref, gain_in, early_ref,
    out_ref, gain_ref, got_ref, window, staged, begins, numbers, flags, spots, shift_ref, doubled, in_sems, sems,
):
    in_early = pltpu.make_async_copy(early_ref, staged, in_sems.at[0])
    in_early.start()
    in_got = pltpu.make_async_copy(got_in, got_ref, in_sems.at[1])
    in_got.start()
    per_peer = got_ref.shape[1]
    n_blocks = gain_ref.shape[0]
    reach = BLOCK + 16
    gain_ref[...] = gain_in[...]
    tabulate(counts, begins, numbers, n_grp)
    for b in range(n_blocks):
        flags[b] = 0
    for h in range(n_grp):
        end = begins[h] + numbers[h]

        def mark(b, _):
            flags[b] = 1
            return 0

        low = lax.div(begins[h] + EARLY_ROWS, BLOCK)
        high = jnp.where(numbers[h] > EARLY_ROWS, lax.div(end - 1, BLOCK) + 1, low)
        lax.fori_loop(low, high, mark, 0)
        if h + SOURCES < n_grp:
            last = lax.div(jnp.maximum(end - 1, 0), BLOCK)

            @pl.when(last == lax.div(begins[h + SOURCES], BLOCK))
            def _():
                flags[last] = 1

    def span(b):
        return pl.ds(pl.multiple_of(b * BLOCK, BLOCK), BLOCK)

    def copy_new(b):
        return pltpu.make_async_copy(staged.at[b], out_ref.at[0, 0, span(b), :], sems.at[b])

    def keep(b, _):
        @pl.when(flags[b] == 0)
        def _():
            copy_new(b).start()

        return 0

    set_up(n_grp, n_pts, counts, owner, slot_ref, weights_ref, spots, shift_ref, doubled)
    window[...] = jnp.zeros_like(window)
    in_early.wait()
    lax.fori_loop(0, n_blocks, keep, 0)
    in_got.wait()
    row = lax.broadcasted_iota(jnp.int32, (BLOCK, EMBED), 0)

    def redo(b, _):
        @pl.when(flags[b] == 1)
        def _():
            base = pl.multiple_of(b * BLOCK, BLOCK)
            first = first_source(begins, numbers, base, n_grp)
            stop = jnp.int32(0)
            for h in range(n_grp):
                stop += jnp.where(begins[h] < base + BLOCK, 1, 0)

            def add(source, x):
                skip = base - begins[source]
                at = jnp.clip((skip >> 4) << 4, 0, per_peer - reach)
                at = pl.multiple_of(at, 16)
                window[BLOCK : BLOCK + reach, :] = got_ref[source, pl.ds(at, reach), :].astype(F32)
                begin = jnp.clip(skip - at, -BLOCK, reach) + BLOCK
                new = window[pl.ds(begin, BLOCK), :]
                return jnp.where((row + skip >= 0) & (row + skip < numbers[source]), new, x)

            x = lax.fori_loop(first, stop, add, jnp.zeros((BLOCK, EMBED), F32))
            parts, gain = factor_rows(x, base, weights_ref, spots, shift_ref, doubled)
            for r in range(ROUNDS):
                staged[b, :, r * BLOCK : (r + 1) * BLOCK] = parts[r]
            gain_ref[pl.ds(b, 1), :] = gain
            copy_new(b).start()

        return 0

    lax.fori_loop(0, n_blocks, redo, 0)

    def finish(b, _):
        copy_new(b).wait()
        return 0

    lax.fori_loop(0, n_blocks, finish, 0)


def late(got, counts, pick_slot, block_owner, weights, gain, early_rows, n_grp, n_pts):
    n_blocks = gain.shape[0]
    smem = pl.BlockSpec(memory_space=pltpu.SMEM)
    vmem = pl.BlockSpec(memory_space=pltpu.VMEM)
    hbm = pl.BlockSpec(memory_space=pltpu.HBM)
    return pl.pallas_call(
        functools.partial(late_kernel, n_grp, n_pts),
        out_shape=(
            jax.ShapeDtypeStruct((1, 1, n_blocks * BLOCK, FACTOR), BF16),
            jax.ShapeDtypeStruct(gain.shape, F32),
        ),
        in_specs=[smem, smem, vmem, hbm, vmem, vmem, hbm],
        out_specs=(hbm, vmem),
        scratch_shapes=[
            pltpu.VMEM(got.shape, BF16),
            pltpu.VMEM((3 * BLOCK + 16, EMBED), F32),
            pltpu.VMEM((n_blocks, BLOCK, FACTOR), BF16),
            pltpu.SMEM((n_grp,), jnp.int32),
            pltpu.SMEM((n_grp,), jnp.int32),
            pltpu.SMEM((n_blocks,), jnp.int32),
            pltpu.VMEM((1, FACTOR), jnp.int32),
            pltpu.VMEM((1, FACTOR), F32),
            pltpu.VMEM((2 * BLOCK, BLOCK), BF16),
            pltpu.SemaphoreType.DMA((2,)),
            pltpu.SemaphoreType.DMA((n_blocks,)),
        ],
        compiler_params=pltpu.CompilerParams(vmem_limit_bytes=58 << 20),
        name="late",
    )(counts, block_owner, pick_slot, got, weights, gain, early_rows)


def per_device(patches, counts, pick_slot, block_owner):
    n_grp, n_pts = lax.axis_size("grp"), lax.axis_size("pts")
    got, weights, rows, gain = exchange(patches, counts, pick_slot, block_owner, n_grp, n_pts)
    rows, gain = late(got, counts, pick_slot, block_owner, weights, gain, rows, n_grp, n_pts)
    return rows, gain.reshape(1, 1, gain.size)


def solution(mesh):
    in_specs = (P("grp", "pts", None, None), P(), P(), P())
    out_specs = (P("grp", "pts", None, None), P("grp", "pts", None))
    return jax.shard_map(
        per_device, mesh=mesh, in_specs=in_specs, out_specs=out_specs, check_vma=False
    )
```

```python
import functools
import math

import jax
import jax.numpy as jnp
from jax import lax
from jax.experimental import pallas as pl
from jax.experimental.pallas import tpu as pltpu
from jax.sharding import PartitionSpec as P

MESH = pl.DeviceIdType.MESH
HIGHEST = lax.Precision.HIGHEST
JITTER = 0.1
EMBED = 128
BLOCK = 128
ROUNDS = 3
FACTOR = ROUNDS * BLOCK
PARTS = 12
PART_ROWS = FACTOR // PARTS
FIRST_ROWS = 256
EARLY_ROWS = 768
SOURCES = 3
EXP_SCALE = math.log2(math.e) / EMBED
F32 = jnp.float32
BF16 = jnp.bfloat16


def dot(a, b, precision=None):
    return jnp.dot(a, b, precision=precision, preferred_element_type=F32)


def dot_nt(a, b, precision=None):
    return lax.dot_general(
        a, b, (((1,), (1,)), ((), ())), precision=precision, preferred_element_type=F32
    )


def halves(x):
    high = x.astype(BF16)
    return high, (x - high.astype(F32)).astype(BF16)


def greet(axis_sizes, place, meanwhile):
    barrier = pltpu.get_barrier_semaphore()
    total = 0
    for axis, size in axis_sizes:
        for d in range(1, size):
            pl.semaphore_signal(barrier, inc=1, device_id=place(axis, d), device_id_type=MESH)
        total += size - 1
    meanwhile()
    pl.semaphore_wait(barrier, total)


def neighbour(n_grp, n_pts):
    group, col = lax.axis_index("grp"), lax.axis_index("pts")

    def place(axis, d):
        if axis == "grp":
            return (lax.rem(group + d, n_grp), col)
        return (group, lax.rem(col + d, n_pts))

    return place


def unit_inverse(a_ref, m_ref):
    sub = lax.broadcasted_iota(jnp.int32, (8, BLOCK), 0)
    m_ref[...] = (
        lax.broadcasted_iota(jnp.int32, (BLOCK, BLOCK), 0)
        == lax.broadcasted_iota(jnp.int32, (BLOCK, BLOCK), 1)
    ).astype(F32)

    def row(x, k):
        return jnp.broadcast_to(x[k : k + 1, :], (8, BLOCK))

    for b in range(BLOCK // 8):
        low = 8 * b
        pa = a_ref[low : low + 8, :]
        pm = m_ref[low : low + 8, :]
        cols = [jnp.broadcast_to(pa[:, low + j : low + j + 1], (8, BLOCK)) for j in range(8)]
        pivots = jnp.ones((8, BLOCK), F32)
        inverses = pivots
        for k in range(8):
            pivot = row(cols[k], k)
            inverse = 1.0 / pivot
            pivots = jnp.where(sub == k, pivot, pivots)
            inverses = jnp.where(sub == k, inverse, inverses)
            if k < 7:
                f = jnp.where(sub > k, cols[k] * inverse, 0.0)
                for j in range(k + 1, 8):
                    cols[j] = cols[j] - f * row(cols[j], k)
                pa = pa - f * row(pa, k)
                pm = pm - f * row(pm, k)
        if b < BLOCK // 8 - 1:
            below = pa.T[low + 8 :, :]
            a_ref[low + 8 :, :] -= dot(below, pa * inverses, HIGHEST)
            m_ref[low + 8 :, :] -= dot(below, pm * inverses, HIGHEST)
        scale = lax.rsqrt(pivots)
        scale = scale * (1.5 - 0.5 * pivots * scale * scale)
        m_ref[low : low + 8, :] = pm * scale


def prepare(blocks, weights_ref, schur, work, inv):
    wide = blocks.astype(F32)
    sq_high, sq_low = halves(wide * wide)
    ones = jnp.ones((EMBED, BLOCK), BF16)
    sq_col = dot(sq_high, ones) + dot(sq_low, ones)
    row_ones = jnp.ones((8, EMBED), BF16)
    sq_row = (dot_nt(row_ones, sq_high) + dot_nt(row_ones, sq_low))[0:1, :]
    weights_ref[2 * FACTOR :, :] = (2.0 * wide).T.astype(BF16)
    eye = (
        lax.broadcasted_iota(jnp.int32, (BLOCK, BLOCK), 0)
        == lax.broadcasted_iota(jnp.int32, (BLOCK, BLOCK), 1)
    )
    def span(i):
        return slice(i * BLOCK, (i + 1) * BLOCK)

    for i in range(ROUNDS):
        for j in range(i + 1):
            inner = dot_nt(blocks[span(i)], blocks[span(j)])
            dist = 2.0 * inner - sq_col[span(i)] - sq_row[:, span(j)]
            part = jnp.exp2(EXP_SCALE * dist)
            if i == j:
                part = part + jnp.where(eye, JITTER, 0.0)
            schur[i, j] = part

    for r in range(ROUNDS):
        work[...] = schur[r, r]
        unit_inverse(work, inv.at[r, r])
        for i in range(r + 1, ROUNDS):
            schur[i, r] = dot_nt(schur[i, r], inv[r, r], HIGHEST)
        for i in range(r + 1, ROUNDS):
            for j in range(r + 1, i + 1):
                schur[i, j] -= dot_nt(schur[i, r], schur[j, r], HIGHEST)

    inv[1, 0] = -dot(inv[1, 1], dot(schur[1, 0], inv[0, 0], HIGHEST), HIGHEST)
    inv[2, 1] = -dot(inv[2, 2], dot(schur[2, 1], inv[1, 1], HIGHEST), HIGHEST)
    inv[2, 0] = -dot(
        inv[2, 2],
        dot(schur[2, 0], inv[0, 0], HIGHEST) + dot(schur[2, 1], inv[1, 0], HIGHEST),
        HIGHEST,
    )
    for i in range(ROUNDS):
        for j in range(ROUNDS):
            if j <= i:
                high, low = halves(inv[i, j].T)
            else:
                high = low = jnp.zeros((BLOCK, BLOCK), BF16)
            weights_ref[span(j), span(i)] = high
            weights_ref[span(ROUNDS + j), span(i)] = low


def segment(counts, col, group, h, start, n_grp):
    odd = start & (n_grp - 1)
    begin = lax.div(start, n_grp) + jnp.where(group < odd, 1, 0)
    first = (group - odd) & (n_grp - 1)
    number = jnp.maximum(lax.div(counts[col, h] - first + n_grp - 1, n_grp), 0)
    return begin, number


def set_up(n_grp, n_pts, counts, owner, slot_ref, weights_ref, spots, shift_ref, doubled):
    group, col = lax.axis_index("grp"), lax.axis_index("pts")
    for r in range(ROUNDS):
        own_group, own_col = lax.div(owner[r], n_pts), lax.rem(owner[r], n_pts)
        begin = jnp.int32(0)
        for h in range(n_grp):
            begin += jnp.where(h < own_group, counts[own_col, h], 0)
        rank = begin + slot_ref[r : r + 1, :]
        here = (own_col == col) & ((rank & (n_grp - 1)) == group)
        spots[0:1, r * BLOCK : (r + 1) * BLOCK] = jnp.where(
            here, rank >> (n_grp.bit_length() - 1), -1
        )
    corner = weights_ref[2 * BLOCK : FACTOR, 2 * BLOCK :]
    doubled[0:BLOCK, :] = corner
    doubled[BLOCK:, :] = corner
    twice = weights_ref[2 * FACTOR :, :].astype(F32)
    high, low = halves(twice * twice)
    ones = jnp.ones((8, EMBED), BF16)
    shift_ref[...] = (-0.25 * EXP_SCALE) * (dot(ones, high) + dot(ones, low))[0:1, :]


def factor_rows(wide, base, weights_ref, spots, shift_ref, doubled):
    rows = wide.shape[0]
    high_ref, low_ref = weights_ref.at[0:FACTOR], weights_ref.at[FACTOR : 2 * FACTOR]
    twice_ref = weights_ref.at[2 * FACTOR :]
    x = wide.astype(BF16)
    sq = jnp.concatenate(halves(wide * wide), axis=1)
    sq = dot(sq, jnp.ones((2 * EMBED, BLOCK), BF16))
    spot = lax.broadcasted_iota(jnp.int32, (rows, BLOCK), 0) + base
    inner = dot(x, twice_ref[...])
    high, low = [], []
    for r in range(ROUNDS):
        at = slice(r * BLOCK, (r + 1) * BLOCK)
        part = jnp.exp2(EXP_SCALE * (inner[:, at] - sq) + shift_ref[0:1, at])
        part = part + jnp.where(spot == spots[0:1, at], JITTER, 0.0)
        a, b = halves(part)
        high.append(a)
        low.append(b)
    both = 2 * BLOCK
    high01 = jnp.concatenate(high[:2], axis=1)
    low01 = jnp.concatenate(low[:2], axis=1)
    first = (
        dot(high01, high_ref[0:both, :])
        + dot(low01, high_ref[0:both, :])
        + dot(high01, low_ref[0:both, :])
    )
    last = (
        dot(jnp.concatenate([high[2], low[2]], axis=1), doubled[...])
        + dot(high[2], low_ref[both:, both:])
    )
    parts = [first[:, 0:BLOCK], first[:, BLOCK:both], first[:, both:] + last]
    square = parts[0] * parts[0] + parts[1] * parts[1] + parts[2] * parts[2]
    square = jnp.concatenate(halves(square), axis=1)
    gain = (1.0 + JITTER) - dot_nt(jnp.ones((8, 2 * BLOCK), BF16), square)[0:1, :]
    return [p.astype(BF16) for p in parts], gain


def tabulate(counts, begins, numbers, n_grp):
    group, col = lax.axis_index("grp"), lax.axis_index("pts")
    start = jnp.int32(0)
    for h in range(n_grp):
        begin, number = segment(counts, col, group, h, start, n_grp)
        begins[h] = begin
        numbers[h] = number
        start += counts[col, h]


def first_source(begins, numbers, base, n_grp):
    source = jnp.int32(0)
    for h in range(n_grp):
        source += jnp.where(begins[h] + numbers[h] <= base, 1, 0)
    return jnp.minimum(source, n_grp - 1)


def exchange_kernel(
    n_grp, n_pts, counts, owner, slot_ref, patches_ref, got_ref, weights_ref, early_ref, gain_ref,
    spread_out, local, staged, points, begins, numbers, spots, shift_ref, doubled, local_sem, out_sems,
    x_ref, send_ref, order, picks_ref, got1, got2, part, gathered, schur, work, inv,
    load_sems, own_sem, *sems,
):
    group, col = lax.axis_index("grp"), lax.axis_index("pts")
    me = group * n_pts + col
    place = neighbour(n_grp, n_pts)
    (s1, r1), (s2, r2), (s3, r3) = sems[0:2], sems[2:4], sems[4:6]
    bulk = sems[6:]
    per_peer = send_ref.shape[1]
    edges = (0, FIRST_ROWS, EARLY_ROWS, per_peer)
    tile = order.shape[0]
    each = tile // n_grp
    loads = load_sems.shape[0]
    load_rows = x_ref.shape[0] // loads
    near_first = sorted(range(1, n_grp), key=lambda d: min(d, n_grp - d))

    def load(i):
        span = pl.ds(i * load_rows, load_rows)
        return pltpu.make_async_copy(patches_ref.at[0, 0, span], x_ref.at[span], load_sems.at[i])

    for i in range(loads):
        load(i).start()

    def set_order():
        start = jnp.int32(0)
        for h in range(n_grp):
            start += jnp.where(h < group, counts[col, h], 0)
        to = lax.broadcasted_iota(jnp.int32, (tile, tile), 0)
        source = (to & (each - 1)) * n_grp + (((to >> (each.bit_length() - 1)) - start) & (n_grp - 1))
        hit = source == lax.broadcasted_iota(jnp.int32, (tile, tile), 1)
        order[...] = hit.astype(F32).astype(BF16)

    def sort_rows(low, high):
        for c in range(low // each, high // each):
            moved = dot(order[...], x_ref[c * tile : (c + 1) * tile, :]).astype(BF16)
            send_ref[:, c * each : (c + 1) * each, :] = moved.reshape(n_grp, each, EMBED)

    def find_picks():
        slots = jnp.full((1, BLOCK), -1, jnp.int32)
        for r in range(ROUNDS):
            slots = jnp.where(owner[r] == me, slot_ref[r : r + 1, :], slots)
        wanted = jnp.broadcast_to(slots, (BLOCK, BLOCK)).T
        wanted -= lax.broadcasted_iota(jnp.int32, (BLOCK, BLOCK), 1)
        unroll = 8

        def look(i, acc):
            for u in range(unroll):
                at = pl.multiple_of((i * unroll + u) * BLOCK, BLOCK)
                hit = (wanted == at).astype(F32).astype(BF16)
                acc += dot(hit, x_ref[pl.ds(at, BLOCK), :])
            return acc

        found = lax.fori_loop(
            0, x_ref.shape[0] // (unroll * BLOCK), look, jnp.zeros((BLOCK, EMBED), F32)
        )
        for r in range(ROUNDS):
            mine = jnp.where(owner[r] == me, found, 0.0).astype(BF16)
            per_round = BLOCK // PART_ROWS
            picks_ref[r * per_round : (r + 1) * per_round] = mine.reshape(per_round, PART_ROWS, EMBED)

    def rows(piece, d):
        span = pl.ds(edges[piece], edges[piece + 1] - edges[piece])
        target = lax.rem(group + d, n_grp)
        return pltpu.make_async_remote_copy(
            src_ref=send_ref.at[target, span],
            dst_ref=got_ref.at[group, span],
            send_sem=bulk[2 * piece].at[d],
            recv_sem=bulk[2 * piece + 1].at[d],
            device_id=place("grp", d),
            device_id_type=MESH,
        )

    def before():
        set_order()
        for i in range(FIRST_ROWS * n_grp // load_rows):
            load(i).wait()
        sort_rows(0, FIRST_ROWS)

    greet((("pts", n_pts), ("grp", n_grp)), place, before)
    for d in near_first:
        rows(0, d).start()
    for i in range(FIRST_ROWS * n_grp // load_rows, loads):
        load(i).wait()
    find_picks()

    def scatter(d):
        target = lax.rem(col + d, n_pts)
        return target, pltpu.make_async_remote_copy(
            src_ref=picks_ref.at[jnp.minimum(target, PARTS - 1)],
            dst_ref=got1.at[d - 1],
            send_sem=s1.at[d],
            recv_sem=r1.at[d],
            device_id=place("pts", d),
            device_id_type=MESH,
        )

    def across(d):
        return pltpu.make_async_remote_copy(
            src_ref=part.at[0],
            dst_ref=got2.at[d - 1],
            send_sem=s2.at[d],
            recv_sem=r2.at[d],
            device_id=place("grp", d),
            device_id_type=MESH,
        )

    def gather(d, owner):
        return pltpu.make_async_remote_copy(
            src_ref=part.at[1],
            dst_ref=gathered.at[owner],
            send_sem=s3.at[d],
            recv_sem=r3.at[d],
            device_id=place("pts", d),
            device_id_type=MESH,
        )

    for d in range(1, n_pts):
        target, copy = scatter(d)

        @pl.when(target < PARTS)
        def _():
            copy.start()

    sort_rows(FIRST_ROWS, per_peer)
    own = pltpu.make_async_copy(send_ref.at[group], got_ref.at[group], own_sem)
    own.start()

    @pl.when(col < PARTS)
    def _():
        acc = picks_ref[jnp.minimum(col, PARTS - 1)].astype(F32)
        for d in range(1, n_pts):
            scatter(d)[1].wait_recv()
            acc += got1[d - 1].astype(F32)
        part[0] = acc.astype(BF16)
        for d in range(1, n_grp):
            across(d).start()

    for piece in (1, 2):
        for d in near_first:
            rows(piece, d).start()

    @pl.when(col < PARTS)
    def _():
        acc = part[0].astype(F32)
        for d in range(1, n_grp):
            across(d).wait_recv()
            acc += got2[d - 1].astype(F32)
        part[1] = acc.astype(BF16)
        for d in range(1, n_pts):
            gather(d, col).start()
        gathered[col] = part[1]

    for d in range(1, n_pts):
        source = lax.rem(col + n_pts - d, n_pts)

        @pl.when(source < PARTS)
        def _():
            gather(d, source).wait_recv()

    prepare(gathered[...].reshape(FACTOR, EMBED), weights_ref, schur, work, inv)
    set_up(n_grp, n_pts, counts, owner, slot_ref, weights_ref, spots, shift_ref, doubled)
    tabulate(counts, begins, numbers, n_grp)
    spread_out[:, 0:BLOCK, :] = jnp.zeros((n_grp, BLOCK, EMBED), F32)
    spread_out[:, BLOCK + EARLY_ROWS :, :] = jnp.zeros((n_grp, BLOCK, EMBED), F32)

    own.wait()
    for piece in (0, 1):
        for d in near_first:
            rows(piece, d).wait_recv()
    fetch = pltpu.make_async_copy(got_ref.at[:, pl.ds(0, EARLY_ROWS)], local, local_sem)
    fetch.start()
    fetch.wait()

    def widen(h, _):
        spread_out[h, BLOCK : BLOCK + EARLY_ROWS, :] = local[h].astype(F32)
        return 0

    lax.fori_loop(0, n_grp, widen, 0)
    row = lax.broadcasted_iota(jnp.int32, (BLOCK, EMBED), 0)
    step_rows = points.shape[0]

    per_step = step_rows // BLOCK

    def out_copy(i):
        span = pl.ds(i * per_step, per_step)
        return pltpu.make_async_copy(staged.at[span], early_ref.at[span], out_sems.at[i])

    def early(i, _):
        base = pl.multiple_of(i * step_rows, step_rows)
        for b in range(step_rows // BLOCK):
            first = first_source(begins, numbers, base + b * BLOCK, n_grp)
            x = jnp.zeros((BLOCK, EMBED), F32)
            for k in range(SOURCES):
                source = jnp.minimum(first + k, n_grp - 1)
                skip = base + b * BLOCK - begins[source]
                limit = jnp.minimum(numbers[source], EARLY_ROWS)
                at = jnp.clip(skip, -BLOCK, EARLY_ROWS) + BLOCK
                new = spread_out[source, pl.ds(at, BLOCK), :]
                x = jnp.where((row + skip >= 0) & (row + skip < limit), new, x)
            points[b * BLOCK : (b + 1) * BLOCK, :] = x
        parts, gain = factor_rows(points[...], base, weights_ref, spots, shift_ref, doubled)
        for b in range(per_step):
            for r in range(ROUNDS):
                staged[i * per_step + b, :, r * BLOCK : (r + 1) * BLOCK] = parts[r][
                    b * BLOCK : (b + 1) * BLOCK, :
                ]
            gain_ref[pl.ds(i * (step_rows // BLOCK) + b, 1), :] = gain[:, b * BLOCK : (b + 1) * BLOCK]
        out_copy(i).start()
        return 0

    lax.fori_loop(0, out_sems.shape[0], early, 0)

    for d in range(1, n_pts):
        target, copy = scatter(d)

        @pl.when(target < PARTS)
        def _():
            copy.wait_send()

    @pl.when(col < PARTS)
    def _():
        for d in range(1, n_grp):
            across(d).wait_send()
        for d in range(1, n_pts):
            gather(d, col).wait_send()

    def finish(i, _):
        out_copy(i).wait()
        return 0

    lax.fori_loop(0, out_sems.shape[0], finish, 0)
    for d in near_first:
        rows(2, d).wait_recv()
    for piece in range(3):
        for d in near_first:
            rows(piece, d).wait_send()


def exchange(patches, counts, pick_slot, block_owner, n_grp, n_pts):
    slots = patches.shape[2]
    shape = (PARTS, PART_ROWS, EMBED)
    square = (ROUNDS, ROUNDS, BLOCK, BLOCK)
    messages = (n_grp, slots // n_grp, EMBED)
    points = slots // 2
    rows = 512
    return pl.pallas_call(
        functools.partial(exchange_kernel, n_grp, n_pts),
        out_shape=(
            jax.ShapeDtypeStruct(messages, BF16),
            jax.ShapeDtypeStruct((2 * FACTOR + EMBED, FACTOR), BF16),
            jax.ShapeDtypeStruct((points // BLOCK, BLOCK, FACTOR), BF16),
            jax.ShapeDtypeStruct((points // BLOCK, BLOCK), F32),
        ),
        in_specs=[
            pl.BlockSpec(memory_space=pltpu.SMEM),
            pl.BlockSpec(memory_space=pltpu.SMEM),
            pl.BlockSpec(memory_space=pltpu.VMEM),
            pl.BlockSpec(memory_space=pltpu.HBM),
        ],
        out_specs=(
            pl.BlockSpec(memory_space=pltpu.HBM),
            pl.BlockSpec(memory_space=pltpu.VMEM),
            pl.BlockSpec(memory_space=pltpu.HBM),
            pl.BlockSpec(memory_space=pltpu.VMEM),
        ),
        scratch_shapes=[
            pltpu.VMEM((n_grp, EARLY_ROWS + 2 * BLOCK, EMBED), F32),
            pltpu.VMEM((n_grp, EARLY_ROWS, EMBED), BF16),
            pltpu.VMEM((points // BLOCK, BLOCK, FACTOR), BF16),
            pltpu.VMEM((rows, EMBED), F32),
            pltpu.SMEM((n_grp,), jnp.int32),
            pltpu.SMEM((n_grp,), jnp.int32),
            pltpu.VMEM((1, FACTOR), jnp.int32),
            pltpu.VMEM((1, FACTOR), F32),
            pltpu.VMEM((2 * BLOCK, BLOCK), BF16),
            pltpu.SemaphoreType.DMA,
            pltpu.SemaphoreType.DMA((points // rows,)),
            pltpu.VMEM((slots, EMBED), BF16),
            pltpu.VMEM(messages, BF16),
            pltpu.VMEM((n_grp * 16, n_grp * 16), BF16),
            pltpu.VMEM(shape, BF16),
            pltpu.VMEM((n_pts - 1,) + shape[1:], BF16),
            pltpu.VMEM((n_grp - 1,) + shape[1:], BF16),
            pltpu.VMEM((2,) + shape[1:], BF16),
            pltpu.VMEM(shape, BF16),
            pltpu.VMEM(square, F32),
            pltpu.VMEM((BLOCK, BLOCK), F32),
            pltpu.VMEM(square, F32),
            pltpu.SemaphoreType.DMA((8,)),
            pltpu.SemaphoreType.DMA,
        ]
        + [pltpu.SemaphoreType.DMA((n,)) for n in (n_pts, n_pts, n_grp, n_grp, n_pts, n_pts)]
        + [pltpu.SemaphoreType.DMA((n_grp,))] * 6,
        compiler_params=pltpu.CompilerParams(
            collective_id=0, has_side_effects=True, vmem_limit_bytes=58 << 20
        ),
        name="exchange",
    )(counts, block_owner, pick_slot, patches)


def late_kernel(
    n_grp, n_pts, counts, owner, slot_ref, got_in, weights_ref, gain_in, early_ref,
    out_ref, gain_ref, got_ref, window, staged, begins, numbers, flags, spots, shift_ref, doubled, in_sems, sems,
):
    shares = in_sems.shape[0] - 1
    share = staged.shape[0] // shares

    def in_early(i):
        span = pl.ds(i * share, share)
        return pltpu.make_async_copy(early_ref.at[span], staged.at[span], in_sems.at[i])

    for i in range(shares):
        in_early(i).start()
    in_got = pltpu.make_async_copy(got_in, got_ref, in_sems.at[shares])
    in_got.start()
    per_peer = got_ref.shape[1]
    n_blocks = gain_ref.shape[0]
    reach = BLOCK + 16
    gain_ref[...] = gain_in[...]
    tabulate(counts, begins, numbers, n_grp)
    for b in range(n_blocks):
        flags[b] = 0
    for h in range(n_grp):
        end = begins[h] + numbers[h]

        def mark(b, _):
            flags[b] = 1
            return 0

        low = lax.div(begins[h] + EARLY_ROWS, BLOCK)
        high = jnp.where(numbers[h] > EARLY_ROWS, lax.div(end - 1, BLOCK) + 1, low)
        lax.fori_loop(low, high, mark, 0)
        if h + SOURCES < n_grp:
            last = lax.div(jnp.maximum(end - 1, 0), BLOCK)

            @pl.when(last == lax.div(begins[h + SOURCES], BLOCK))
            def _():
                flags[last] = 1

    def span(b):
        return pl.ds(pl.multiple_of(b * BLOCK, BLOCK), BLOCK)

    def copy_new(b):
        return pltpu.make_async_copy(staged.at[b], out_ref.at[0, 0, span(b), :], sems.at[b])

    def keep(b, _):
        @pl.when(flags[b] == 0)
        def _():
            copy_new(b).start()

        return 0

    set_up(n_grp, n_pts, counts, owner, slot_ref, weights_ref, spots, shift_ref, doubled)
    window[...] = jnp.zeros_like(window)
    for i in range(shares):
        in_early(i).wait()
        lax.fori_loop(i * share, (i + 1) * share, keep, 0)
    in_got.wait()
    row = lax.broadcasted_iota(jnp.int32, (BLOCK, EMBED), 0)

    def redo(b, _):
        @pl.when(flags[b] == 1)
        def _():
            base = pl.multiple_of(b * BLOCK, BLOCK)
            first = first_source(begins, numbers, base, n_grp)
            stop = jnp.int32(0)
            for h in range(n_grp):
                stop += jnp.where(begins[h] < base + BLOCK, 1, 0)

            def add(source, x):
                skip = base - begins[source]
                at = jnp.clip((skip >> 4) << 4, 0, per_peer - reach)
                at = pl.multiple_of(at, 16)
                window[BLOCK : BLOCK + reach, :] = got_ref[source, pl.ds(at, reach), :].astype(F32)
                begin = jnp.clip(skip - at, -BLOCK, reach) + BLOCK
                new = window[pl.ds(begin, BLOCK), :]
                return jnp.where((row + skip >= 0) & (row + skip < numbers[source]), new, x)

            x = lax.fori_loop(first, stop, add, jnp.zeros((BLOCK, EMBED), F32))
            parts, gain = factor_rows(x, base, weights_ref, spots, shift_ref, doubled)
            for r in range(ROUNDS):
                staged[b, :, r * BLOCK : (r + 1) * BLOCK] = parts[r]
            gain_ref[pl.ds(b, 1), :] = gain
            copy_new(b).start()

        return 0

    lax.fori_loop(0, n_blocks, redo, 0)

    def finish(b, _):
        copy_new(b).wait()
        return 0

    lax.fori_loop(0, n_blocks, finish, 0)


def late(got, counts, pick_slot, block_owner, weights, gain, early_rows, n_grp, n_pts):
    n_blocks = gain.shape[0]
    smem = pl.BlockSpec(memory_space=pltpu.SMEM)
    vmem = pl.BlockSpec(memory_space=pltpu.VMEM)
    hbm = pl.BlockSpec(memory_space=pltpu.HBM)
    return pl.pallas_call(
        functools.partial(late_kernel, n_grp, n_pts),
        out_shape=(
            jax.ShapeDtypeStruct((1, 1, n_blocks * BLOCK, FACTOR), BF16),
            jax.ShapeDtypeStruct(gain.shape, F32),
        ),
        in_specs=[smem, smem, vmem, hbm, vmem, vmem, hbm],
        out_specs=(hbm, vmem),
        scratch_shapes=[
            pltpu.VMEM(got.shape, BF16),
            pltpu.VMEM((3 * BLOCK + 16, EMBED), F32),
            pltpu.VMEM((n_blocks, BLOCK, FACTOR), BF16),
            pltpu.SMEM((n_grp,), jnp.int32),
            pltpu.SMEM((n_grp,), jnp.int32),
            pltpu.SMEM((n_blocks,), jnp.int32),
            pltpu.VMEM((1, FACTOR), jnp.int32),
            pltpu.VMEM((1, FACTOR), F32),
            pltpu.VMEM((2 * BLOCK, BLOCK), BF16),
            pltpu.SemaphoreType.DMA((5,)),
            pltpu.SemaphoreType.DMA((n_blocks,)),
        ],
        compiler_params=pltpu.CompilerParams(vmem_limit_bytes=58 << 20),
        name="late",
    )(counts, block_owner, pick_slot, got, weights, gain, early_rows)


def per_device(patches, counts, pick_slot, block_owner):
    n_grp, n_pts = lax.axis_size("grp"), lax.axis_size("pts")
    got, weights, rows, gain = exchange(patches, counts, pick_slot, block_owner, n_grp, n_pts)
    rows, gain = late(got, counts, pick_slot, block_owner, weights, gain, rows, n_grp, n_pts)
    return rows, gain.reshape(1, 1, gain.size)


def solution(mesh):
    in_specs = (P("grp", "pts", None, None), P(), P(), P())
    out_specs = (P("grp", "pts", None, None), P("grp", "pts", None))
    return jax.shard_map(
        per_device, mesh=mesh, in_specs=in_specs, out_specs=out_specs, check_vma=False
    )
```
